256 devices in a mesh: stream: 16 (over z, core), cross: 16 (over x, y).
Axes of the slice: x: 4, y: 4, z: 8, core: 2. Of those that a mesh axis runs over, the one named last changes fastest.
Arguments:
- forcing: float32 [16, 16, 8, 128, 128], P('stream', 'cross'), may hold values from -6 to 6
- block_fine: float32 [16, 16, 8, 128, 128], P('stream', 'cross'), may hold values from -1 to 2
- couple_fine: float32 [16, 16, 8, 128, 128], P('stream', 'cross'), may hold values from -1 to 1
- pattern_fine: int32 [16, 16, 8], P('stream', 'cross'), may hold values from 0 to 7
- restrict_fine: int32 [16, 16, 256], P('stream', 'cross'), may hold values from 0 to 159
- landing_one: int32 [16, 16, 32], P('stream', 'cross'), may hold values from 0 to 127
- block_mid: float32 [16, 16, 4, 128, 128], P('stream', 'cross'), may hold values from -1 to 2
- couple_mid: float32 [16, 16, 4, 128, 128], P('stream', 'cross'), may hold values from -1 to 1
- pattern_mid: int32 [16, 16, 4], P('stream', 'cross'), may hold values from 0 to 3
- restrict_mid: int32 [16, 16, 128], P('stream', 'cross'), may hold values from 0 to 79
- landing_two: int32 [16, 16, 16], P('stream', 'cross'), may hold values from 0 to 63
- block_low: float32 [16, 16, 2, 128, 128], P('stream', 'cross'), may hold values from -1 to 2
- owner_cells: int32 [16, 16, 64], P('stream', 'cross'), may hold values from 0 to 127
- coarse_inverse: float32 [16, 512, 512], P('stream', 'cross'), may hold values from -1 to 2
Outputs:
- smooth_fine: float32 [16, 16, 8, 128, 128], P('stream', 'cross')
- smooth_mid: float32 [16, 16, 4, 128, 128], P('stream', 'cross')
- smooth_low: float32 [16, 16, 2, 128, 128], P('stream', 'cross')
- coarse_fix: float32 [16, 512, 128], P('stream', 'cross')
The draws below stay inside these ranges and needn't reach their ends.
All inputs are finite; a program needn't handle non-finite values.
Results may differ from the reference program's by a relative error of at most 0.0003.
Values sent between devices are 32-bit elements; how exact they have to be, the bound alone decides.
A program may use at most 64 MiB of HBM per device.

```python
import math
import jax
import jax.numpy as jnp
from jax import lax

BCELL = 32
NB0 = 8
R = 128
CHEB = 6
UNK = 128
NB1 = 4
NB2 = 2
C0 = 256
M1 = 128
S1 = 32
M2 = 64
S2 = 16
M3 = 128
N_STREAM = 16
N_CROSS = 16


def noisy_matrix(key, shape, fan, with_identity):
    scale = 0.5 / math.sqrt(fan)
    noise = jax.random.truncated_normal(key, -4.0, 4.0, shape, jnp.float32) * scale
    if with_identity:
        rows = lax.broadcasted_iota(jnp.int32, shape, len(shape) - 2)
        columns = lax.broadcasted_iota(jnp.int32, shape, len(shape) - 1)
        noise = noise + (rows == columns).astype(jnp.float32)
    return noise


def draw_block_fine(key, part):
    return noisy_matrix(jax.random.fold_in(key, 11), (N_STREAM, N_CROSS, NB0, UNK, UNK), 2 * UNK, True)


def draw_couple_fine(key, part):
    return noisy_matrix(jax.random.fold_in(key, 12), (N_STREAM, N_CROSS, NB0, UNK, UNK), 2 * UNK, False)


def draw_block_mid(key, part):
    return noisy_matrix(jax.random.fold_in(key, 21), (N_STREAM, N_CROSS, NB1, UNK, UNK), 2 * UNK, True)


def draw_couple_mid(key, part):
    return noisy_matrix(jax.random.fold_in(key, 22), (N_STREAM, N_CROSS, NB1, UNK, UNK), 2 * UNK, False)


def draw_block_low(key, part):
    return noisy_matrix(jax.random.fold_in(key, 31), (N_STREAM, N_CROSS, NB2, UNK, UNK), UNK, True)


def draw_coarse_inverse(key, part):
    return noisy_matrix(jax.random.fold_in(key, 41), (N_STREAM, 4 * M3, 4 * M3), 4 * M3, True)


def touch_ends(entries, own_key, smallest, top_value):
    longest = entries.shape.index(max(entries.shape))
    spots = []
    for shift in (0, 1):
        where = [jax.random.randint(jax.random.fold_in(own_key, axis), (), 0, length) for axis, length in enumerate(entries.shape)]
        where[longest] = (where[longest] + shift) % entries.shape[longest]
        spots.append(tuple(where))
    return entries.at[spots[0]].set(smallest).at[spots[1]].set(top_value)


def steps_of(rng, dims, shards, smallest, largest):
    def one(position, shards_of):
        steps = jax.random.uniform(jax.random.fold_in(jax.random.fold_in(rng, 6), position), (shards_of,), jnp.float32, smallest / len(shards), largest / len(shards))
        return jnp.repeat(jnp.exp(steps), dims[position] // shards_of).reshape((-1,) + (1,) * (len(dims) - position - 1))

    factor_of = one(*shards[0])
    for cut in shards[1:]:
        factor_of = factor_of * one(*cut)
    return factor_of


def normal_values(own_key, shape, width, bound, pieces=(), dtype=jnp.bfloat16):
    factor_of = steps_of(own_key, shape, pieces, -0.22, 0.18) if pieces else 1.0
    entries = jax.random.normal(own_key, shape, jnp.float32) * width * factor_of
    return jnp.minimum(jnp.maximum(entries, -bound), bound).astype(dtype)


def setup_inputs(seed: int = 0) -> dict:
    splits = jax.random.split(jax.random.key(seed), 15)
    return {
        "forcing": normal_values(splits[0], (N_STREAM, N_CROSS, NB0, UNK, R), 1.0, 6.0, ((0, 16), (1, 16)), jnp.float32),
        "block_fine": draw_block_fine(jax.random.fold_in(splits[14], 71), 0),
        "couple_fine": draw_couple_fine(jax.random.fold_in(splits[14], 71), 0),
        "pattern_fine": touch_ends(jax.random.randint(splits[3], (N_STREAM, N_CROSS, NB0), 0, NB0), jax.random.fold_in(splits[3], 1), 0, NB0 - 1).astype(jnp.int32),
        "restrict_fine": touch_ends(jax.random.randint(splits[4], (N_STREAM, N_CROSS, C0), 0, M1 + S1), jax.random.fold_in(splits[4], 1), 0, (M1 + S1) - 1).astype(jnp.int32),
        "landing_one": touch_ends(jax.random.randint(splits[5], (N_STREAM, N_CROSS, S1), 0, M1), jax.random.fold_in(splits[5], 1), 0, M1 - 1).astype(jnp.int32),
        "block_mid": draw_block_mid(jax.random.fold_in(splits[14], 71), 0),
        "couple_mid": draw_couple_mid(jax.random.fold_in(splits[14], 71), 0),
        "pattern_mid": touch_ends(jax.random.randint(splits[8], (N_STREAM, N_CROSS, NB1), 0, NB1), jax.random.fold_in(splits[8], 1), 0, NB1 - 1).astype(jnp.int32),
        "restrict_mid": touch_ends(jax.random.randint(splits[9], (N_STREAM, N_CROSS, M1), 0, M2 + S2), jax.random.fold_in(splits[9], 1), 0, (M2 + S2) - 1).astype(jnp.int32),
        "landing_two": touch_ends(jax.random.randint(splits[10], (N_STREAM, N_CROSS, S2), 0, M2), jax.random.fold_in(splits[10], 1), 0, M2 - 1).astype(jnp.int32),
        "block_low": draw_block_low(jax.random.fold_in(splits[14], 71), 0),
        "owner_cells": touch_ends(jax.random.randint(splits[12], (N_STREAM, N_CROSS, M2), 0, M3), jax.random.fold_in(splits[12], 1), 0, M3 - 1).astype(jnp.int32),
        "coarse_inverse": draw_coarse_inverse(jax.random.fold_in(splits[14], 71), 0),
    }


centre = 1.0
spread = 0.5
coarse_weight = 0.5


def apply_blocks(diagonal_blocks, coupling, pattern, vector):
    result = jnp.einsum("bij,bjr->bir", diagonal_blocks, vector, precision=lax.Precision.HIGHEST)
    if coupling is not None:
        result = result + jnp.einsum("bij,bjr->bir", coupling, jnp.take(vector, pattern, axis=0), precision=lax.Precision.HIGHEST)
    return result


def chebyshev(diagonal_blocks, coupling, pattern, source):
    ratio_bound = centre / spread
    momentum = 1.0 / ratio_bound
    update = source / centre
    answer = update
    residual = source
    for sweep_index in range(CHEB):
        residual = residual - apply_blocks(diagonal_blocks, coupling, pattern, update)
        momentum_next = 1.0 / (2.0 * ratio_bound - momentum)
        update = (momentum_next * momentum) * update + (2.0 * momentum_next / spread) * residual
        answer = answer + update
        momentum = momentum_next
    residual = residual - apply_blocks(diagonal_blocks, coupling, pattern, update)
    return answer, residual


def cell_rows(vector, cell_count):
    block_count, unknowns, columns = vector.shape
    return vector.reshape(block_count, 4, cell_count, columns).transpose(0, 2, 1, 3).reshape(block_count * cell_count, 4 * columns)


def block_rows(rows, cell_count):
    total_rows, width_all = rows.shape
    columns = width_all // 4
    block_count = total_rows // cell_count
    return rows.reshape(block_count, cell_count, 4, columns).transpose(0, 2, 1, 3).reshape(block_count, 4 * cell_count, columns)


def restrict(residual, cell_map, segments):
    return coarse_weight * jax.ops.segment_sum(cell_rows(residual, BCELL), cell_map, num_segments=segments)


def add_landed(owned_rows, arrived, landing):
    return owned_rows + jax.ops.segment_sum(arrived, landing, num_segments=owned_rows.shape[0])


def reference(forcing, block_fine, couple_fine, pattern_fine, restrict_fine, landing_one, block_mid, couple_mid, pattern_mid, restrict_mid, landing_two, block_low, owner_cells, coarse_inverse):
    streams = forcing.shape[0]
    crosses = forcing.shape[1]

    def flatten_tiles(array):
        return array.reshape((streams * crosses,) + array.shape[2:])

    def unflatten(array):
        return array.reshape((streams, crosses) + array.shape[1:])

    def level_fine(items):
        answer, residual = chebyshev(items[1], items[2], items[3], items[0])
        return answer, restrict(residual, items[4], M1 + S1)

    answer_fine, partial_value = lax.map(level_fine, tuple(flatten_tiles(a) for a in (forcing, block_fine, couple_fine, pattern_fine, restrict_fine)))
    partial_value = unflatten(partial_value)
    arrived = jnp.roll(partial_value[:, :, M1:], 1, axis=0)
    source = jax.vmap(jax.vmap(add_landed))(partial_value[:, :, :M1], arrived, landing_one)
    source_mid = flatten_tiles(source)

    def level_mid(items):
        answer, residual = chebyshev(items[1], items[2], items[3], block_rows(items[0], BCELL))
        return answer, restrict(residual, items[4], M2 + S2)

    answer_mid, partial_two = lax.map(level_mid, (source_mid,) + tuple(flatten_tiles(a) for a in (block_mid, couple_mid, pattern_mid, restrict_mid)))
    partial_two = unflatten(partial_two)
    arrived_two = jnp.roll(partial_two[:, :, M2:], 1, axis=0)
    source_two = flatten_tiles(jax.vmap(jax.vmap(add_landed))(partial_two[:, :, :M2], arrived_two, landing_two))

    def level_low(items):
        answer, residual = chebyshev(items[1], None, None, block_rows(items[0], BCELL))
        return answer, restrict(residual, items[2], M3)

    answer_low, partial_three = lax.map(level_low, (source_two, flatten_tiles(block_low), flatten_tiles(owner_cells)))
    partial_three = unflatten(partial_three)
    coarse_source = jnp.sum(partial_three, axis=1)
    coarse_source = coarse_source.reshape(streams, 4 * M3, coarse_source.shape[2] // 4)
    coarse_fix = jnp.einsum("sij,sjr->sir", coarse_inverse, coarse_source, precision=lax.Precision.HIGHEST)
    return (unflatten(answer_fine), unflatten(answer_mid), unflatten(answer_low), coarse_fix)
```

```python
import functools

import jax
import jax.numpy as jnp
from jax import lax
from jax.experimental import pallas as pl
from jax.experimental.pallas import tpu as pltpu
from jax.sharding import PartitionSpec as P

MESH = pl.DeviceIdType.MESH
BCELL = 32
CHEB = 6
M1 = 128
S1 = 32
M2 = 64
S2 = 16
UNK = 128
R = 128
NB0 = 8
NB1 = 4
NB2 = 2
COARSE = 512

centre = 1.0
spread = 0.5
coarse_weight = 0.5

f32 = jnp.float32
bf16 = jnp.bfloat16


def coefficients():
    ratio_bound = centre / spread
    momentum = 1.0 / ratio_bound
    pairs = []
    for _ in range(CHEB):
        momentum_next = 1.0 / (2.0 * ratio_bound - momentum)
        pairs.append((momentum_next * momentum, 2.0 * momentum_next / spread))
        momentum = momentum_next
    return pairs


STEPS = coefficients()


def dot(a, b):
    return jnp.dot(a, b, preferred_element_type=f32)


def split(value):
    high = value.astype(bf16)
    return high, (value - high.astype(f32)).astype(bf16)


def halves(value):
    return jnp.concatenate(split(value), axis=1)


def product(matrix, vector):
    rows = matrix.shape[0] // 2
    both = dot(matrix[:rows], vector)
    return both[:, :R] + both[:, R:] + dot(matrix[rows:], vector[:, :R])


def stack_parts(target, b, column, value):
    high, low = split(value)
    target[b, :UNK, column : column + UNK] = high
    target[b, UNK:, column : column + UNK] = low


def smoothing(blocks, pattern, source, operator, vectors, answer, residual, update, answer_ready, finish):
    for step in range(CHEB + 1):
        now, later = vectors[step % 2], vectors[(step + 1) % 2]
        for b in range(blocks):
            own = now[b]
            if pattern is not None:
                own = jnp.concatenate([own, now[pattern[b]]], axis=0)
            left = (source[b] if step == 0 else residual[b]) - product(operator[b], own)
            if step == CHEB:
                finish(b, left)
                continue
            residual[b] = left
            keep, gain = STEPS[step]
            changed = keep * (source[b] if step == 0 else update[b]) + gain * left
            if step < CHEB - 1:
                update[b] = changed
            answer[b] = (source[b] if step == 0 else answer[b]) + changed
            later[b] = halves(changed)
        if step == CHEB - 1:
            answer_ready()


def selector(rows, targets, weight):
    wanted = lax.broadcasted_iota(jnp.int32, (rows, targets.shape[1]), 0)
    return jnp.where(wanted == targets, jnp.float32(weight), jnp.float32(0.0)).astype(bf16)


def gathered(matrix, vector):
    both = dot(matrix, vector)
    return both[:, :R] + both[:, R:]


def kernel(
    n_stream,
    n_cross,
    pattern_fine,
    pattern_mid,
    restrict_fine,
    landing_one,
    restrict_mid,
    landing_two,
    owner_cells,
    forcing,
    block_fine,
    couple_fine,
    block_mid,
    couple_mid,
    block_low,
    inverse,
    out_fine,
    out_mid,
    out_low,
    out_fix,
    f_fine,
    d_fine,
    c_fine,
    a_fine,
    v_fine0,
    v_fine1,
    x_fine,
    r_fine,
    u_fine,
    p_fine,
    d_mid,
    c_mid,
    a_mid,
    f_mid,
    v_mid0,
    v_mid1,
    x_mid,
    r_mid,
    u_mid,
    p_mid,
    d_low,
    a_low,
    e_low,
    v_low0,
    v_low1,
    x_low,
    r_low,
    u_low,
    pq_low,
    f_low,
    p_low,
    y_low,
    inv,
    inv_parts,
    send_one,
    got_one,
    send_two,
    got_two,
    partial,
    slots,
    share,
    coarse,
    fix,
    load_f,
    load_d,
    load_c,
    load_rest,
    store_sem,
    one_send,
    one_recv,
    two_send,
    two_recv,
    rs_send,
    rs_recv,
    ag_send,
    ag_recv,
):
    me_s = lax.axis_index("stream")
    me_c = lax.axis_index("cross")
    ahead = lax.rem(me_s + 1, n_stream)
    behind = lax.rem(me_s + n_stream - 1, n_stream)
    share_rows = COARSE // n_cross

    def start(source, target, sem):
        copy = pltpu.make_async_copy(source, target, sem)
        copy.start()
        return copy

    copy_f = start(forcing, f_fine, load_f)
    copies_d = []
    copies_c = []
    for b in range(NB0):
        copies_d.append(start(block_fine.at[b], d_fine.at[b], load_d.at[b]))
        copies_c.append(start(couple_fine.at[b], c_fine.at[b], load_c.at[b]))
    copy_dm = start(block_mid, d_mid, load_rest.at[0])
    copy_cm = start(couple_mid, c_mid, load_rest.at[1])
    copy_dl = start(block_low, d_low, load_rest.at[2])
    copy_inv = start(inverse, inv, load_rest.at[3])

    barrier = pltpu.get_barrier_semaphore()
    for peer in (ahead, behind):
        pl.semaphore_signal(barrier, inc=1, device_id={"stream": peer}, device_id_type=MESH)
    for offset in range(1, n_cross):
        peer = lax.rem(me_c + offset, n_cross)
        pl.semaphore_signal(barrier, inc=1, device_id={"cross": peer}, device_id_type=MESH)

    copy_f.wait()
    for b in range(NB0):
        v_fine0[b] = halves(f_fine[b])
    for b in range(NB0):
        copies_d[b].wait()
        stack_parts(a_fine, b, 0, d_fine[b])
        copies_c[b].wait()
        stack_parts(a_fine, b, UNK, c_fine[b])

    stores = []

    def finish_fine(b, value):
        p_fine[b] = halves(value)

    smoothing(
        NB0,
        pattern_fine,
        f_fine,
        a_fine,
        (v_fine0, v_fine1),
        x_fine,
        r_fine,
        u_fine,
        lambda: stores.append(start(x_fine, out_fine, store_sem.at[0])),
        finish_fine,
    )

    pl.semaphore_wait(barrier, n_cross + 1)

    def to_next(c, source, target, send_sems, recv_sems):
        return pltpu.make_async_remote_copy(
            src_ref=source.at[c],
            dst_ref=target.at[c],
            send_sem=send_sems.at[c],
            recv_sem=recv_sems.at[c],
            device_id={"stream": ahead},
            device_id_type=MESH,
        )

    pick = selector(M1 + S1, restrict_fine[...], coarse_weight)
    to_one = []
    for c in range(4):
        rows = p_fine[:, c * BCELL : (c + 1) * BCELL, :].reshape(NB0 * BCELL, 2 * R)
        sums = gathered(pick, rows)
        send_one[c] = sums[M1:]
        copy = to_next(c, send_one, got_one, one_send, one_recv)
        copy.start()
        to_one.append(copy)
        for b in range(NB1):
            f_mid[b, c * BCELL : (c + 1) * BCELL, :] = sums[b * BCELL : (b + 1) * BCELL]

    copy_dm.wait()
    copy_cm.wait()
    for b in range(NB1):
        stack_parts(a_mid, b, 0, d_mid[b])
        stack_parts(a_mid, b, UNK, c_mid[b])
    copy_dl.wait()
    row = lax.broadcasted_iota(jnp.int32, (UNK, UNK), 0)
    column = lax.broadcasted_iota(jnp.int32, (UNK, UNK), 1)
    for b in range(NB2):
        stack_parts(a_low, b, 0, d_low[b])
        e_low[b] = jnp.where(row == column, jnp.float32(1.0), jnp.float32(0.0))
        v_low0[b] = halves(e_low[b])

    def finish_low(b, value):
        high, low = split(x_low[b])
        pq_low[b, 0:UNK] = high
        pq_low[b, UNK : 2 * UNK] = low
        high, low = split(value)
        pq_low[b, 2 * UNK : 3 * UNK] = high
        pq_low[b, 3 * UNK :] = low

    smoothing(
        NB2,
        None,
        e_low,
        a_low,
        (v_low0, v_low1),
        x_low,
        r_low,
        u_low,
        lambda: None,
        finish_low,
    )
    land = selector(M1, landing_one[...], 1.0)

    for c in range(4):
        to_one[c].wait_recv()
        landed = gathered(land, halves(got_one[c]))
        for b in range(NB1):
            cells = slice(c * BCELL, (c + 1) * BCELL)
            source = f_mid[b, cells, :] + landed[b * BCELL : (b + 1) * BCELL]
            f_mid[b, cells, :] = source
            v_mid0[b, cells, :] = halves(source)

    def finish_mid(b, value):
        p_mid[b] = halves(value)

    smoothing(
        NB1,
        pattern_mid,
        f_mid,
        a_mid,
        (v_mid0, v_mid1),
        x_mid,
        r_mid,
        u_mid,
        lambda: stores.append(start(x_mid, out_mid, store_sem.at[1])),
        finish_mid,
    )

    pick = selector(M2 + S2, restrict_mid[...], coarse_weight)
    to_two = []
    for c in range(4):
        rows = p_mid[:, c * BCELL : (c + 1) * BCELL, :].reshape(NB1 * BCELL, 2 * R)
        sums = gathered(pick, rows)
        send_two[c] = sums[M2:]
        copy = to_next(c, send_two, got_two, two_send, two_recv)
        copy.start()
        to_two.append(copy)
        for b in range(NB2):
            f_low[b, c * BCELL : (c + 1) * BCELL, :] = sums[b * BCELL : (b + 1) * BCELL]

    copy_inv.wait()
    high, low = split(inv[...])
    inv_parts[:share_rows] = high
    inv_parts[share_rows:] = low
    owners = owner_cells[...] * 4
    targets = jnp.concatenate(
        [owners[:, b * BCELL : (b + 1) * BCELL] + c for b in range(NB2) for c in range(4)],
        axis=1,
    )
    land = selector(M2, landing_two[...], 1.0)

    for c in range(4):
        to_two[c].wait_recv()
        landed = gathered(land, halves(got_two[c]))
        for b in range(NB2):
            cells = slice(c * BCELL, (c + 1) * BCELL)
            f_low[b, cells, :] = f_low[b, cells, :] + landed[b * BCELL : (b + 1) * BCELL]

    for b in range(NB2):
        vector = halves(f_low[b])
        y_low[b] = product(pq_low[b, : 2 * UNK], vector)
        p_low[b] = halves(product(pq_low[b, 2 * UNK :], vector))
    stores.append(start(y_low, out_low, store_sem.at[2]))

    pick = selector(COARSE, targets, coarse_weight)
    rows = p_low[...].reshape(NB2 * UNK, 2 * R)
    partial[...] = gathered(pick, rows).reshape(n_cross, share_rows, R)

    scattered = []
    for offset in range(1, n_cross):
        peer = lax.rem(me_c + offset, n_cross)
        copy = pltpu.make_async_remote_copy(
            src_ref=partial.at[peer],
            dst_ref=slots.at[offset],
            send_sem=rs_send.at[offset],
            recv_sem=rs_recv.at[offset],
            device_id={"cross": peer},
            device_id_type=MESH,
        )
        copy.start()
        scattered.append(copy)
    total = partial[me_c]
    for offset in range(1, n_cross):
        scattered[offset - 1].wait_recv()
        total = total + slots[offset]
    share[...] = total

    spread_out = []
    for offset in range(1, n_cross):
        peer = lax.rem(me_c + offset, n_cross)
        copy = pltpu.make_async_remote_copy(
            src_ref=share,
            dst_ref=coarse.at[me_c],
            send_sem=ag_send.at[offset],
            recv_sem=ag_recv.at[offset],
            device_id={"cross": peer},
            device_id_type=MESH,
        )
        copy.start()
        spread_out.append(copy)
    coarse[me_c] = total
    for offset in range(1, n_cross):
        origin = lax.rem(me_c + n_cross - offset, n_cross)
        pltpu.make_async_remote_copy(
            src_ref=share,
            dst_ref=coarse.at[origin],
            send_sem=ag_send.at[offset],
            recv_sem=ag_recv.at[offset],
            device_id={"cross": lax.rem(me_c + offset, n_cross)},
            device_id_type=MESH,
        ).wait_recv()

    fix[...] = product(inv_parts[...], halves(coarse[...].reshape(COARSE, R)))
    stores.append(start(fix, out_fix, store_sem.at[3]))
    for copy in to_one + to_two + scattered + spread_out:
        copy.wait_send()
    for copy in stores:
        copy.wait()


def on_device(n_stream, n_cross, forcing, block_fine, couple_fine, pattern_fine, restrict_fine, landing_one,
              block_mid, couple_mid, pattern_mid, restrict_mid, landing_two, block_low, owner_cells, coarse_inverse):
    share_rows = COARSE // n_cross
    smem = pl.BlockSpec(memory_space=pltpu.SMEM)
    vmem = pl.BlockSpec(memory_space=pltpu.VMEM)
    anywhere = pl.BlockSpec(memory_space=pl.ANY)

    def vector(blocks):
        return pltpu.VMEM((blocks, UNK, R), f32)

    def parts(blocks):
        return pltpu.VMEM((blocks, UNK, 2 * R), bf16)

    def dma(*shape):
        return pltpu.SemaphoreType.DMA(shape)

    fine, mid, low, fix = pl.pallas_call(
        functools.partial(kernel, n_stream, n_cross),
        out_shape=(
            jax.ShapeDtypeStruct((NB0, UNK, R), f32),
            jax.ShapeDtypeStruct((NB1, UNK, R), f32),
            jax.ShapeDtypeStruct((NB2, UNK, R), f32),
            jax.ShapeDtypeStruct((share_rows, R), f32),
        ),
        in_specs=[smem] * 2 + [vmem] * 5 + [anywhere] * 7,
        out_specs=(anywhere,) * 4,
        scratch_shapes=[
            vector(NB0),
            vector(NB0),
            vector(NB0),
            pltpu.VMEM((NB0, 2 * UNK, 2 * UNK), bf16),
            parts(NB0),
            parts(NB0),
            vector(NB0),
            vector(NB0),
            vector(NB0),
            parts(NB0),
            vector(NB1),
            vector(NB1),
            pltpu.VMEM((NB1, 2 * UNK, 2 * UNK), bf16),
            vector(NB1),
            parts(NB1),
            parts(NB1),
            vector(NB1),
            vector(NB1),
            vector(NB1),
            parts(NB1),
            vector(NB2),
            pltpu.VMEM((NB2, 2 * UNK, UNK), bf16),
            vector(NB2),
            parts(NB2),
            parts(NB2),
            vector(NB2),
            vector(NB2),
            vector(NB2),
            pltpu.VMEM((NB2, 4 * UNK, UNK), bf16),
            vector(NB2),
            parts(NB2),
            vector(NB2),
            pltpu.VMEM((share_rows, COARSE), f32),
            pltpu.VMEM((2 * share_rows, COARSE), bf16),
            pltpu.VMEM((4, S1, R), f32),
            pltpu.VMEM((4, S1, R), f32),
            pltpu.VMEM((4, S2, R), f32),
            pltpu.VMEM((4, S2, R), f32),
            pltpu.VMEM((n_cross, share_rows, R), f32),
            pltpu.VMEM((n_cross, share_rows, R), f32),
            pltpu.VMEM((share_rows, R), f32),
            pltpu.VMEM((n_cross, share_rows, R), f32),
            pltpu.VMEM((share_rows, R), f32),
            pltpu.SemaphoreType.DMA,
            dma(NB0),
            dma(NB0),
            dma(4),
            dma(4),
            dma(4),
            dma(4),
            dma(4),
            dma(4),
            dma(n_cross),
            dma(n_cross),
            dma(n_cross),
            dma(n_cross),
        ],
        compiler_params=pltpu.CompilerParams(
            collective_id=0, has_side_effects=True, vmem_limit_bytes=48 << 20
        ),
        name="vcycle",
    )(
        pattern_fine.reshape(NB0),
        pattern_mid.reshape(NB1),
        restrict_fine.reshape(1, -1),
        landing_one.reshape(1, -1),
        restrict_mid.reshape(1, -1),
        landing_two.reshape(1, -1),
        owner_cells.reshape(1, -1),
        forcing[0, 0],
        block_fine[0, 0],
        couple_fine[0, 0],
        block_mid[0, 0],
        couple_mid[0, 0],
        block_low[0, 0],
        coarse_inverse[0],
    )
    return fine[None, None], mid[None, None], low[None, None], fix[None]


def solution(mesh):
    tile = P("stream", "cross", None, None, None)
    table = P("stream", "cross", None)
    return jax.shard_map(
        functools.partial(on_device, mesh.shape["stream"], mesh.shape["cross"]),
        mesh=mesh,
        in_specs=(tile, tile, tile, table, table, table, tile, tile, table, table, table, tile, table, table),
        out_specs=(tile, tile, tile, table),
        check_vma=False,
    )
```

```python
import functools
import math
import types

import jax
import jax.numpy as jnp
from jax import lax
from jax.experimental import pallas as pl
from jax.experimental.pallas import tpu as pltpu
from jax.sharding import PartitionSpec as P

MESH = pl.DeviceIdType.MESH
BCELL = 32
CHEB = 6
M1 = 128
S1 = 32
M2 = 64
S2 = 16
UNK = 128
R = 128
NB0 = 8
NB1 = 4
NB2 = 2
COARSE = 512
BARRIER_AFTER = 2

centre = 1.0
spread = 0.5
coarse_weight = 0.5

f32 = jnp.float32
bf16 = jnp.bfloat16


def coefficients():
    ratio_bound = centre / spread
    momentum = 1.0 / ratio_bound
    pairs = []
    for _ in range(CHEB):
        momentum_next = 1.0 / (2.0 * ratio_bound - momentum)
        pairs.append((momentum_next * momentum, 2.0 * momentum_next / spread))
        momentum = momentum_next
    return pairs


STEPS = coefficients()


def dot(a, b):
    return jnp.dot(a, b, preferred_element_type=f32)


def split(value):
    high = value.astype(bf16)
    return high, (value - high.astype(f32)).astype(bf16)


def halves(value):
    return jnp.concatenate(split(value), axis=1)


def product(matrix, vector):
    rows = matrix.shape[0] // 2
    both = dot(matrix[:rows], vector)
    return both[:, :R] + both[:, R:] + dot(matrix[rows:], vector[:, :R])


def stack_parts(target, b, column, value):
    high, low = split(value)
    target[b, :UNK, column : column + UNK] = high
    target[b, UNK:, column : column + UNK] = low


def smoothing(blocks, pattern, source, operator, vectors, answer, residual, update, after, finish):
    for step in range(CHEB + 1):
        now, later = vectors[step % 2], vectors[(step + 1) % 2]
        for b in range(blocks):
            own = now[b]
            if pattern is not None:
                own = jnp.concatenate([own, now[pattern[b]]], axis=0)
            left = (source[b] if step == 0 else residual[b]) - product(operator[b], own)
            if step == CHEB:
                finish(b, left)
                continue
            residual[b] = left
            keep, gain = STEPS[step]
            changed = keep * (source[b] if step == 0 else update[b]) + gain * left
            if step < CHEB - 1:
                update[b] = changed
            answer[b] = (source[b] if step == 0 else answer[b]) + changed
            later[b] = halves(changed)
        after(step)


def selector(rows, targets, weight):
    wanted = lax.broadcasted_iota(jnp.int32, (rows, targets.shape[1]), 0)
    return jnp.where(wanted == targets, jnp.float32(weight), jnp.float32(0.0)).astype(bf16)


def gathered(matrix, vector):
    both = dot(matrix, vector)
    return both[:, :R] + both[:, R:]


def scratch_of(side):
    rows = COARSE // (side * side)

    def vector(blocks):
        return pltpu.VMEM((blocks, UNK, R), f32)

    def operator(blocks):
        return pltpu.VMEM((blocks, 2 * UNK, 2 * UNK), bf16)

    def parts(blocks):
        return pltpu.VMEM((blocks, UNK, 2 * R), bf16)

    def table(width):
        return pltpu.VMEM((1, width), jnp.int32)

    def dma(*shape):
        return pltpu.SemaphoreType.DMA(shape)

    return dict(
        pat_fine=pltpu.SMEM((1, NB0), jnp.int32),
        pat_mid=pltpu.SMEM((1, NB1), jnp.int32),
        map_fine=table(2 * M1),
        map_land_one=table(S1),
        map_mid=table(M1),
        map_land_two=table(S2),
        map_owner=table(M2),
        f_fine=vector(NB0),
        d_fine=vector(NB0),
        c_fine=vector(NB0),
        r_fine=vector(NB0),
        u_fine=vector(NB0),
        a_fine=operator(NB0),
        v_fine0=parts(NB0),
        v_fine1=parts(NB0),
        p_fine=parts(NB0),
        f_mid=vector(NB1),
        d_mid=vector(NB1),
        c_mid=vector(NB1),
        r_mid=vector(NB1),
        u_mid=vector(NB1),
        a_mid=operator(NB1),
        v_mid0=parts(NB1),
        v_mid1=parts(NB1),
        p_mid=parts(NB1),
        f_low=vector(NB2),
        d_low=vector(NB2),
        e_low=vector(NB2),
        x_low=vector(NB2),
        r_low=vector(NB2),
        u_low=vector(NB2),
        a_low=pltpu.VMEM((NB2, 2 * UNK, UNK), bf16),
        pq_low=pltpu.VMEM((NB2, 4 * UNK, UNK), bf16),
        v_low0=parts(NB2),
        v_low1=parts(NB2),
        p_low=parts(NB2),
        inv=pltpu.VMEM((side, side, rows, COARSE), f32),
        send_one=pltpu.VMEM((4, S1, R), f32),
        got_one=pltpu.VMEM((4, S1, R), f32),
        send_two=pltpu.VMEM((4, S2, R), f32),
        got_two=pltpu.VMEM((4, S2, R), f32),
        sums=pltpu.VMEM((COARSE, 2 * R), bf16),
        shares=pltpu.VMEM((side, side, rows, R), f32),
        slots=pltpu.VMEM((side, side, rows, R), f32),
        load_small=dma(7),
        load_d=dma(NB0),
        load_c=dma(NB0),
        load_rest=dma(5),
        one_send=dma(4),
        one_recv=dma(4),
        two_send=dma(4),
        two_recv=dma(4),
        in_send=dma(2, side),
        in_recv=dma(2, side),
        on_send=dma(2, side),
        on_recv=dma(2, side),
        rs_send=dma(side, side),
        rs_recv=dma(side, side),
    )


def kernel(
    n_stream,
    side,
    names,
    pattern_fine,
    pattern_mid,
    restrict_fine,
    landing_one,
    restrict_mid,
    landing_two,
    owner_cells,
    forcing,
    block_fine,
    couple_fine,
    block_mid,
    couple_mid,
    block_low,
    inverse,
    x_fine,
    x_mid,
    y_low,
    fix,
    *scratch,
):
    k = types.SimpleNamespace(**dict(zip(names, scratch)))
    n_cross = side * side
    rows = COARSE // n_cross
    half = rows // 2
    me_s = lax.axis_index("stream")
    me_c = lax.axis_index("cross")
    x = me_c // side
    y = lax.rem(me_c, side)
    ahead = lax.rem(me_s + 1, n_stream)
    behind = lax.rem(me_s + n_stream - 1, n_stream)

    def plus(a, offset):
        return lax.rem(a + offset, side)

    def start(source, target, sem):
        copy = pltpu.make_async_copy(source, target, sem)
        copy.start()
        return copy

    def to_cross(source, target, send, recv, peer_x, peer_y):
        return pltpu.make_async_remote_copy(
            src_ref=source,
            dst_ref=target,
            send_sem=send,
            recv_sem=recv,
            device_id={"cross": peer_x * side + peer_y},
            device_id_type=MESH,
        )

    def to_next(c, source, target, send_sems, recv_sems):
        return pltpu.make_async_remote_copy(
            src_ref=source.at[c],
            dst_ref=target.at[c],
            send_sem=send_sems.at[c],
            recv_sem=recv_sems.at[c],
            device_id={"stream": ahead},
            device_id_type=MESH,
        )

    copy_f = start(forcing, k.f_fine, k.load_rest.at[4])
    copies = []
    for b in range(NB0):
        copies.append(start(block_fine.at[b], k.d_fine.at[b], k.load_d.at[b]))
        copies.append(start(couple_fine.at[b], k.c_fine.at[b], k.load_c.at[b]))
    tables = (
        (pattern_fine, k.pat_fine),
        (pattern_mid, k.pat_mid),
        (restrict_fine, k.map_fine),
        (landing_one, k.map_land_one),
        (restrict_mid, k.map_mid),
        (landing_two, k.map_land_two),
        (owner_cells, k.map_owner),
    )
    small = [start(source, target, k.load_small.at[i]) for i, (source, target) in enumerate(tables)]
    inv = k.inv
    copy_inv = pltpu.make_async_copy(inverse, inv.at[x, y], k.load_rest.at[3])
    copy_inv.start()
    copy_dm = start(block_mid, k.d_mid, k.load_rest.at[0])
    copy_cm = start(couple_mid, k.c_mid, k.load_rest.at[1])
    copy_dl = start(block_low, k.d_low, k.load_rest.at[2])

    barrier = pltpu.get_barrier_semaphore()
    for peer in (ahead, behind):
        pl.semaphore_signal(barrier, inc=1, device_id={"stream": peer}, device_id_type=MESH)
    for offset in range(1, n_cross):
        peer = lax.rem(me_c + offset, n_cross)
        pl.semaphore_signal(barrier, inc=1, device_id={"cross": peer}, device_id_type=MESH)

    copy_f.wait()
    for b in range(NB0):
        k.v_fine0[b] = halves(k.f_fine[b])
    for b in range(NB0):
        copies[2 * b].wait()
        stack_parts(k.a_fine, b, 0, k.d_fine[b])
        copies[2 * b + 1].wait()
        stack_parts(k.a_fine, b, UNK, k.c_fine[b])
    for copy in small:
        copy.wait()
    copy_inv.wait()

    legs = (slice(0, half), slice(half, rows))
    first, second = [], []

    def first_leg():
        for o in range(1, side):
            first.append(to_cross(
                inv.at[x, y, legs[0]], inv.at[x, y, legs[0]],
                k.in_send.at[0, o], k.in_recv.at[0, o], plus(x, o), y,
            ))
            first.append(to_cross(
                inv.at[x, y, legs[1]], inv.at[x, y, legs[1]],
                k.in_send.at[1, o], k.in_recv.at[1, o], x, plus(y, o),
            ))
        for copy in first:
            copy.start()

    def first_leg_arrived():
        for o in range(1, side):
            back_x, back_y = plus(x, side - o), plus(y, side - o)
            to_cross(
                inv.at[back_x, y, legs[0]], inv.at[back_x, y, legs[0]],
                k.in_send.at[0, o], k.in_recv.at[0, o], plus(x, o), y,
            ).wait_recv()
            to_cross(
                inv.at[x, back_y, legs[1]], inv.at[x, back_y, legs[1]],
                k.in_send.at[1, o], k.in_recv.at[1, o], x, plus(y, o),
            ).wait_recv()

    def second_leg():
        for o in range(1, side):
            second.append(to_cross(
                inv.at[:, y, legs[0]], inv.at[:, y, legs[0]],
                k.on_send.at[0, o], k.on_recv.at[0, o], x, plus(y, o),
            ))
            second.append(to_cross(
                inv.at[x, :, legs[1]], inv.at[x, :, legs[1]],
                k.on_send.at[1, o], k.on_recv.at[1, o], plus(x, o), y,
            ))
        for copy in second:
            copy.start()

    def second_leg_arrived():
        for o in range(1, side):
            back_x, back_y = plus(x, side - o), plus(y, side - o)
            to_cross(
                inv.at[:, back_y, legs[0]], inv.at[:, back_y, legs[0]],
                k.on_send.at[0, o], k.on_recv.at[0, o], x, plus(y, o),
            ).wait_recv()
            to_cross(
                inv.at[back_x, :, legs[1]], inv.at[back_x, :, legs[1]],
                k.on_send.at[1, o], k.on_recv.at[1, o], plus(x, o), y,
            ).wait_recv()

    def after_fine(step):
        if step == BARRIER_AFTER:
            pl.semaphore_wait(barrier, n_cross + 1)
            first_leg()

    def finish_fine(b, value):
        k.p_fine[b] = halves(value)

    smoothing(
        NB0, [k.pat_fine[0, b] for b in range(NB0)], k.f_fine, k.a_fine, (k.v_fine0, k.v_fine1),
        x_fine, k.r_fine, k.u_fine, after_fine, finish_fine,
    )

    pick = selector(M1 + S1, k.map_fine[...], coarse_weight)
    to_one = []
    for c in range(4):
        cells = slice(c * BCELL, (c + 1) * BCELL)
        sums = gathered(pick, k.p_fine[:, cells, :].reshape(NB0 * BCELL, 2 * R))
        k.send_one[c] = sums[M1:]
        copy = to_next(c, k.send_one, k.got_one, k.one_send, k.one_recv)
        copy.start()
        to_one.append(copy)
        for b in range(NB1):
            k.f_mid[b, cells, :] = sums[b * BCELL : (b + 1) * BCELL]

    copy_dm.wait()
    copy_cm.wait()
    for b in range(NB1):
        stack_parts(k.a_mid, b, 0, k.d_mid[b])
        stack_parts(k.a_mid, b, UNK, k.c_mid[b])
    first_leg_arrived()
    second_leg()
    copy_dl.wait()
    row = lax.broadcasted_iota(jnp.int32, (UNK, UNK), 0)
    column = lax.broadcasted_iota(jnp.int32, (UNK, UNK), 1)
    for b in range(NB2):
        stack_parts(k.a_low, b, 0, k.d_low[b])
        k.e_low[b] = jnp.where(row == column, jnp.float32(1.0), jnp.float32(0.0))
        k.v_low0[b] = halves(k.e_low[b])

    def finish_low(b, value):
        high, low = split(k.x_low[b])
        k.pq_low[b, 0:UNK] = high
        k.pq_low[b, UNK : 2 * UNK] = low
        high, low = split(value)
        k.pq_low[b, 2 * UNK : 3 * UNK] = high
        k.pq_low[b, 3 * UNK :] = low

    smoothing(
        NB2, None, k.e_low, k.a_low, (k.v_low0, k.v_low1),
        k.x_low, k.r_low, k.u_low, lambda step: None, finish_low,
    )
    land = selector(M1, k.map_land_one[...], 1.0)

    for c in range(4):
        cells = slice(c * BCELL, (c + 1) * BCELL)
        to_one[c].wait_recv()
        landed = gathered(land, halves(k.got_one[c]))
        for b in range(NB1):
            source = k.f_mid[b, cells, :] + landed[b * BCELL : (b + 1) * BCELL]
            k.f_mid[b, cells, :] = source
            k.v_mid0[b, cells, :] = halves(source)

    def finish_mid(b, value):
        k.p_mid[b] = halves(value)

    smoothing(
        NB1, [k.pat_mid[0, b] for b in range(NB1)], k.f_mid, k.a_mid, (k.v_mid0, k.v_mid1),
        x_mid, k.r_mid, k.u_mid, lambda step: None, finish_mid,
    )

    pick = selector(M2 + S2, k.map_mid[...], coarse_weight)
    to_two = []
    for c in range(4):
        cells = slice(c * BCELL, (c + 1) * BCELL)
        sums = gathered(pick, k.p_mid[:, cells, :].reshape(NB1 * BCELL, 2 * R))
        k.send_two[c] = sums[M2:]
        copy = to_next(c, k.send_two, k.got_two, k.two_send, k.two_recv)
        copy.start()
        to_two.append(copy)
        for b in range(NB2):
            k.f_low[b, cells, :] = sums[b * BCELL : (b + 1) * BCELL]

    owners = k.map_owner[...] * 4
    targets = jnp.concatenate(
        [owners[:, b * BCELL : (b + 1) * BCELL] + c for b in range(NB2) for c in range(4)],
        axis=1,
    )
    land = selector(M2, k.map_land_two[...], 1.0)

    for c in range(4):
        cells = slice(c * BCELL, (c + 1) * BCELL)
        to_two[c].wait_recv()
        landed = gathered(land, halves(k.got_two[c]))
        for b in range(NB2):
            k.f_low[b, cells, :] = k.f_low[b, cells, :] + landed[b * BCELL : (b + 1) * BCELL]

    for b in range(NB2):
        vector = halves(k.f_low[b])
        y_low[b] = product(k.pq_low[b, : 2 * UNK], vector)
        k.p_low[b] = halves(product(k.pq_low[b, 2 * UNK :], vector))

    pick = selector(COARSE, targets, coarse_weight)
    k.sums[...] = halves(gathered(pick, k.p_low[...].reshape(NB2 * UNK, 2 * R)))

    second_leg_arrived()
    sums = k.sums[...]
    offsets = [(a, b) for a in range(side) for b in range(side) if a or b]
    offsets.sort(key=lambda o: -(min(o[0], side - o[0]) + min(o[1], side - o[1])))

    def part(px, py):
        return product(jnp.concatenate(split(inv[px, py]), axis=0), sums)

    scattered = []
    for a, b in offsets:
        px, py = plus(x, a), plus(y, b)
        k.shares[a, b] = part(px, py)
        copy = to_cross(
            k.shares.at[a, b], k.slots.at[a, b], k.rs_send.at[a, b], k.rs_recv.at[a, b], px, py
        )
        copy.start()
        scattered.append(copy)
    total = part(x, y)
    for (a, b), copy in reversed(list(zip(offsets, scattered))):
        copy.wait_recv()
        total = total + k.slots[a, b]
    fix[...] = total
    for copy in to_one + to_two + first + second + scattered:
        copy.wait_send()


def write(*refs):
    count = len(refs) // 2
    sems = refs[-1]
    copies = [pltpu.make_async_copy(refs[i], refs[count + i], sems.at[i]) for i in range(count)]
    for copy in copies:
        copy.start()
    for copy in copies:
        copy.wait()


def on_device(n_stream, n_cross, forcing, block_fine, couple_fine, pattern_fine, restrict_fine, landing_one,
              block_mid, couple_mid, pattern_mid, restrict_mid, landing_two, block_low, owner_cells, coarse_inverse):
    side = math.isqrt(n_cross)
    rows = COARSE // n_cross
    anywhere = pl.BlockSpec(memory_space=pl.ANY)
    hbm = pl.BlockSpec(memory_space=pltpu.HBM)
    scratch = scratch_of(side)
    shapes = (
        jax.ShapeDtypeStruct((NB0, UNK, R), f32),
        jax.ShapeDtypeStruct((NB1, UNK, R), f32),
        jax.ShapeDtypeStruct((NB2, UNK, R), f32),
        jax.ShapeDtypeStruct((rows, R), f32),
    )
    made = pl.pallas_call(
        functools.partial(kernel, n_stream, side, tuple(scratch)),
        out_shape=shapes,
        in_specs=[hbm] * 14,
        out_specs=(pl.BlockSpec(memory_space=pltpu.VMEM),) * 4,
        scratch_shapes=list(scratch.values()),
        compiler_params=pltpu.CompilerParams(
            collective_id=0, has_side_effects=True, vmem_limit_bytes=48 << 20
        ),
        name="vcycle",
    )(*(pltpu.with_memory_space_constraint(v, pltpu.HBM) for v in (
        pattern_fine[0],
        pattern_mid[0],
        restrict_fine[0],
        landing_one[0],
        restrict_mid[0],
        landing_two[0],
        owner_cells[0],
        forcing[0, 0],
        block_fine[0, 0],
        couple_fine[0, 0],
        block_mid[0, 0],
        couple_mid[0, 0],
        block_low[0, 0],
        coarse_inverse[0],
        )))
    fine, mid, low, fix = pl.pallas_call(
        write,
        out_shape=shapes,
        in_specs=[pl.BlockSpec(memory_space=pltpu.VMEM)] * 4,
        out_specs=(hbm,) * 4,
        scratch_shapes=[pltpu.SemaphoreType.DMA((4,))],
        name="write",
    )(*(pltpu.with_memory_space_constraint(v, pltpu.VMEM) for v in made))
    return fine[None, None], mid[None, None], low[None, None], fix[None]


def solution(mesh):
    tile = P("stream", "cross", None, None, None)
    table = P("stream", "cross", None)
    return jax.shard_map(
        functools.partial(on_device, mesh.shape["stream"], mesh.shape["cross"]),
        mesh=mesh,
        in_specs=(tile, tile, tile, table, table, table, tile, tile, table, table, table, tile, table, table),
        out_specs=(tile, tile, tile, table),
        check_vma=False,
    )
```

```python
import functools
import math
import types

import jax
import jax.numpy as jnp
from jax import lax
from jax.experimental import pallas as pl
from jax.experimental.pallas import tpu as pltpu
from jax.sharding import PartitionSpec as P

MESH = pl.DeviceIdType.MESH
BCELL = 32
CHEB = 6
M1 = 128
S1 = 32
M2 = 64
S2 = 16
UNK = 128
R = 128
NB0 = 8
NB1 = 4
NB2 = 2
COARSE = 512
BARRIER_AFTER = 0

centre = 1.0
spread = 0.5
coarse_weight = 0.5

f32 = jnp.float32
bf16 = jnp.bfloat16


def coefficients():
    ratio_bound = centre / spread
    momentum = 1.0 / ratio_bound
    pairs = []
    for _ in range(CHEB):
        momentum_next = 1.0 / (2.0 * ratio_bound - momentum)
        pairs.append((momentum_next * momentum, 2.0 * momentum_next / spread))
        momentum = momentum_next
    return pairs


STEPS = coefficients()


def dot(a, b):
    return jnp.dot(a, b, preferred_element_type=f32)


def split(value):
    high = value.astype(bf16)
    return high, (value - high.astype(f32)).astype(bf16)


def halves(value):
    return jnp.concatenate(split(value), axis=1)


def product(matrix, vector):
    rows = matrix.shape[0] // 2
    both = dot(matrix[:rows], vector)
    return both[:, :R] + both[:, R:] + dot(matrix[rows:], vector[:, :R])


def stack_parts(target, b, column, value):
    high, low = split(value)
    target[b, :UNK, column : column + UNK] = high
    target[b, UNK:, column : column + UNK] = low


def smoothing(blocks, pattern, source, operator, vectors, answer, residual, update, after, finish):
    for step in range(CHEB + 1):
        now, later = vectors[step % 2], vectors[(step + 1) % 2]
        for b in range(blocks):
            own = now[b]
            if pattern is not None:
                own = jnp.concatenate([own, now[pattern[b]]], axis=0)
            left = (source[b] if step == 0 else residual[b]) - product(operator[b], own)
            if step == CHEB:
                finish(b, left)
                continue
            residual[b] = left
            keep, gain = STEPS[step]
            changed = keep * (source[b] if step == 0 else update[b]) + gain * left
            if step < CHEB - 1:
                update[b] = changed
            answer[b] = (source[b] if step == 0 else answer[b]) + changed
            later[b] = halves(changed)
        after(step)


def selector(rows, targets, weight):
    wanted = lax.broadcasted_iota(jnp.int32, (rows, targets.shape[1]), 0)
    return jnp.where(wanted == targets, jnp.float32(weight), jnp.float32(0.0)).astype(bf16)


def gathered(matrix, vector):
    both = dot(matrix, vector)
    return both[:, :R] + both[:, R:]


def scratch_of(side):
    rows = COARSE // (side * side)

    def vector(blocks):
        return pltpu.VMEM((blocks, UNK, R), f32)

    def operator(blocks):
        return pltpu.VMEM((blocks, 2 * UNK, 2 * UNK), bf16)

    def parts(blocks):
        return pltpu.VMEM((blocks, UNK, 2 * R), bf16)

    def table(width):
        return pltpu.VMEM((1, width), jnp.int32)

    def dma(*shape):
        return pltpu.SemaphoreType.DMA(shape)

    return dict(
        pat_fine=pltpu.SMEM((1, NB0), jnp.int32),
        pat_mid=pltpu.SMEM((1, NB1), jnp.int32),
        map_fine=table(2 * M1),
        map_land_one=table(S1),
        map_mid=table(M1),
        map_land_two=table(S2),
        map_owner=table(M2),
        f_fine=vector(NB0),
        d_fine=vector(NB0),
        c_fine=vector(NB0),
        r_fine=vector(NB0),
        u_fine=vector(NB0),
        a_fine=operator(NB0),
        v_fine0=parts(NB0),
        v_fine1=parts(NB0),
        p_fine=parts(NB0),
        f_mid=vector(NB1),
        d_mid=vector(NB1),
        c_mid=vector(NB1),
        r_mid=vector(NB1),
        u_mid=vector(NB1),
        a_mid=operator(NB1),
        v_mid0=parts(NB1),
        v_mid1=parts(NB1),
        p_mid=parts(NB1),
        f_low=vector(NB2),
        d_low=vector(NB2),
        e_low=vector(NB2),
        x_low=vector(NB2),
        r_low=vector(NB2),
        u_low=vector(NB2),
        a_low=pltpu.VMEM((NB2, 2 * UNK, UNK), bf16),
        pq_low=pltpu.VMEM((NB2, 4 * UNK, UNK), bf16),
        v_low0=parts(NB2),
        v_low1=parts(NB2),
        p_low=parts(NB2),
        inv=pltpu.VMEM((side, side, rows, COARSE), f32),
        send_one=pltpu.VMEM((4, S1, R), f32),
        got_one=pltpu.VMEM((4, S1, R), f32),
        send_two=pltpu.VMEM((4, S2, R), f32),
        got_two=pltpu.VMEM((4, S2, R), f32),
        inv_parts=pltpu.VMEM((2 * COARSE, COARSE), bf16),
        w_parts=pltpu.VMEM((2 * COARSE, NB2 * UNK), bf16),
        shares=pltpu.VMEM((side * side, rows, R), f32),
        slots=pltpu.VMEM((side * side, rows, R), f32),
        load_small=dma(7),
        load_d=dma(2),
        load_c=dma(2),
        load_rest=dma(5),
        one_send=dma(4),
        one_recv=dma(4),
        two_send=dma(4),
        two_recv=dma(4),
        in_send=dma(2, side),
        in_recv=dma(2, side),
        on_send=dma(2, side, side),
        on_recv=dma(2, side, side),
        rs_send=dma(side * side),
        rs_recv=dma(side * side),
    )


def kernel(
    n_stream,
    side,
    names,
    pattern_fine,
    pattern_mid,
    restrict_fine,
    landing_one,
    restrict_mid,
    landing_two,
    owner_cells,
    forcing,
    block_fine,
    couple_fine,
    block_mid,
    couple_mid,
    block_low,
    inverse,
    x_fine,
    x_mid,
    y_low,
    fix,
    *scratch,
):
    k = types.SimpleNamespace(**dict(zip(names, scratch)))
    n_cross = side * side
    rows = COARSE // n_cross
    half = rows // 2
    me_s = lax.axis_index("stream")
    me_c = lax.axis_index("cross")
    x = me_c // side
    y = lax.rem(me_c, side)
    ahead = lax.rem(me_s + 1, n_stream)
    behind = lax.rem(me_s + n_stream - 1, n_stream)

    def plus(a, offset):
        return lax.rem(a + offset, side)

    def start(source, target, sem):
        copy = pltpu.make_async_copy(source, target, sem)
        copy.start()
        return copy

    def to_cross(source, target, send, recv, peer_x, peer_y):
        return pltpu.make_async_remote_copy(
            src_ref=source,
            dst_ref=target,
            send_sem=send,
            recv_sem=recv,
            device_id={"cross": peer_x * side + peer_y},
            device_id_type=MESH,
        )

    def to_next(c, source, target, send_sems, recv_sems):
        return pltpu.make_async_remote_copy(
            src_ref=source.at[c],
            dst_ref=target.at[c],
            send_sem=send_sems.at[c],
            recv_sem=recv_sems.at[c],
            device_id={"stream": ahead},
            device_id_type=MESH,
        )

    copy_f = start(forcing, k.f_fine, k.load_rest.at[4])
    copies = []
    for i in range(2):
        part = pl.ds(i * NB0 // 2, NB0 // 2)
        copies.append(start(block_fine.at[part], k.d_fine.at[part], k.load_d.at[i]))
        copies.append(start(couple_fine.at[part], k.c_fine.at[part], k.load_c.at[i]))

    barrier = pltpu.get_barrier_semaphore()
    for peer in (ahead, behind):
        pl.semaphore_signal(barrier, inc=1, device_id={"stream": peer}, device_id_type=MESH)
    for o in range(1, side):
        for peer in (plus(x, o) * side + y, x * side + plus(y, o)):
            pl.semaphore_signal(barrier, inc=1, device_id={"cross": peer}, device_id_type=MESH)

    tables = (
        (pattern_fine, k.pat_fine),
        (restrict_fine, k.map_fine),
        (pattern_mid, k.pat_mid),
        (landing_one, k.map_land_one),
        (restrict_mid, k.map_mid),
        (landing_two, k.map_land_two),
        (owner_cells, k.map_owner),
    )
    small = [start(source, target, k.load_small.at[i]) for i, (source, target) in enumerate(tables)]
    inv = k.inv
    copy_inv = start(inverse, inv.at[x, y], k.load_rest.at[3])
    copy_dm = start(block_mid, k.d_mid, k.load_rest.at[0])
    copy_cm = start(couple_mid, k.c_mid, k.load_rest.at[1])
    copy_dl = start(block_low, k.d_low, k.load_rest.at[2])

    copy_f.wait()
    for b in range(NB0):
        k.v_fine0[b] = halves(k.f_fine[b])
    for i in range(2):
        copies[2 * i].wait()
        copies[2 * i + 1].wait()
        for b in range(i * NB0 // 2, (i + 1) * NB0 // 2):
            stack_parts(k.a_fine, b, 0, k.d_fine[b])
            stack_parts(k.a_fine, b, UNK, k.c_fine[b])
    for copy in small:
        copy.wait()
    copy_inv.wait()

    legs = (slice(0, half), slice(half, rows))
    first, second = [], []

    def first_leg():
        for o in (2, 1, 3):
            first.append(to_cross(inv.at[x, y], inv.at[x, y], k.in_send.at[0, o], k.in_recv.at[0, o], plus(x, o), y))
            first.append(to_cross(inv.at[x, y], inv.at[x, y], k.in_send.at[1, o], k.in_recv.at[1, o], x, plus(y, o)))
        for copy in first:
            copy.start()

    def second_leg():
        for o in (1, 3, 2):
            back_x, back_y = plus(x, side - o), plus(y, side - o)
            to_cross(
                inv.at[back_x, y], inv.at[back_x, y], k.in_send.at[0, o], k.in_recv.at[0, o], plus(x, o), y
            ).wait_recv()
            to_cross(
                inv.at[x, back_y], inv.at[x, back_y], k.in_send.at[1, o], k.in_recv.at[1, o], x, plus(y, o)
            ).wait_recv()
            for p in (2, 1, 3):
                block = inv.at[back_x, y, legs[0]]
                copy = to_cross(block, block, k.on_send.at[0, o, p], k.on_recv.at[0, o, p], x, plus(y, p))
                copy.start()
                second.append(copy)
                block = inv.at[x, back_y, legs[1]]
                copy = to_cross(block, block, k.on_send.at[1, o, p], k.on_recv.at[1, o, p], plus(x, p), y)
                copy.start()
                second.append(copy)

    def second_leg_arrived():
        for o in (1, 3, 2):
            for p in (2, 1, 3):
                block = inv.at[plus(x, side - o), plus(y, side - p), legs[0]]
                to_cross(block, block, k.on_send.at[0, o, p], k.on_recv.at[0, o, p], x, plus(y, p)).wait_recv()
                block = inv.at[plus(x, side - p), plus(y, side - o), legs[1]]
                to_cross(block, block, k.on_send.at[1, o, p], k.on_recv.at[1, o, p], plus(x, p), y).wait_recv()

    def after_fine(step):
        if step == BARRIER_AFTER:
            pl.semaphore_wait(barrier, 2 * side)
            first_leg()

    def finish_fine(b, value):
        k.p_fine[b] = halves(value)

    smoothing(
        NB0, [k.pat_fine[0, b] for b in range(NB0)], k.f_fine, k.a_fine, (k.v_fine0, k.v_fine1),
        x_fine, k.r_fine, k.u_fine, after_fine, finish_fine,
    )

    def component(p, c):
        blocks = p.shape[0]
        return p[:, c * BCELL : (c + 1) * BCELL, :].reshape(blocks * BCELL, 2 * R)

    def send_straddling(p, table, owned, straddling, target, got, send_sems, recv_sems):
        pick = selector(straddling, table - owned, coarse_weight)
        for c in range(4):
            target[c] = gathered(pick, component(p, c))
        sent = [to_next(c, target, got, send_sems, recv_sems) for c in range(4)]
        for copy in sent:
            copy.start()
        return sent

    def keep_owned(p, table, owned, target):
        pick = selector(owned, table, coarse_weight)
        for c in range(4):
            sums = gathered(pick, component(p, c))
            for b in range(owned // BCELL):
                target[b, c * BCELL : (c + 1) * BCELL, :] = sums[b * BCELL : (b + 1) * BCELL]

    to_one = send_straddling(
        k.p_fine, k.map_fine[...], M1, S1, k.send_one, k.got_one, k.one_send, k.one_recv
    )
    second_leg()
    keep_owned(k.p_fine, k.map_fine[...], M1, k.f_mid)

    copy_dm.wait()
    copy_cm.wait()
    for b in range(NB1):
        stack_parts(k.a_mid, b, 0, k.d_mid[b])
        stack_parts(k.a_mid, b, UNK, k.c_mid[b])
    copy_dl.wait()
    row = lax.broadcasted_iota(jnp.int32, (UNK, UNK), 0)
    column = lax.broadcasted_iota(jnp.int32, (UNK, UNK), 1)
    for b in range(NB2):
        stack_parts(k.a_low, b, 0, k.d_low[b])
        k.e_low[b] = jnp.where(row == column, jnp.float32(1.0), jnp.float32(0.0))
        k.v_low0[b] = halves(k.e_low[b])

    def finish_low(b, value):
        high, low = split(k.x_low[b])
        k.pq_low[b, 0:UNK] = high
        k.pq_low[b, UNK : 2 * UNK] = low
        high, low = split(value)
        k.pq_low[b, 2 * UNK : 3 * UNK] = high
        k.pq_low[b, 3 * UNK :] = low

    smoothing(
        NB2, None, k.e_low, k.a_low, (k.v_low0, k.v_low1),
        k.x_low, k.r_low, k.u_low, lambda step: None, finish_low,
    )
    land = selector(M1, k.map_land_one[...], 1.0)

    for copy in to_one:
        copy.wait_recv()
    for c in range(4):
        cells = slice(c * BCELL, (c + 1) * BCELL)
        landed = gathered(land, halves(k.got_one[c]))
        for b in range(NB1):
            source = k.f_mid[b, cells, :] + landed[b * BCELL : (b + 1) * BCELL]
            k.f_mid[b, cells, :] = source
            k.v_mid0[b, cells, :] = halves(source)

    def finish_mid(b, value):
        k.p_mid[b] = halves(value)

    smoothing(
        NB1, [k.pat_mid[0, b] for b in range(NB1)], k.f_mid, k.a_mid, (k.v_mid0, k.v_mid1),
        x_mid, k.r_mid, k.u_mid, lambda step: None, finish_mid,
    )

    to_two = send_straddling(
        k.p_mid, k.map_mid[...], M2, S2, k.send_two, k.got_two, k.two_send, k.two_recv
    )
    keep_owned(k.p_mid, k.map_mid[...], M2, k.f_low)
    land = selector(M2, k.map_land_two[...], 1.0)

    owners = k.map_owner[...] * 4
    targets = jnp.concatenate(
        [owners[:, b * BCELL : (b + 1) * BCELL] + c for b in range(NB2) for c in range(4)],
        axis=1,
    )
    pick = selector(COARSE, targets, coarse_weight)
    offsets = [(a, b) for a in range(side) for b in range(side)]
    offsets.sort(key=lambda o: -(min(o[0], side - o[0]) + min(o[1], side - o[1])))
    second_leg_arrived()
    for i, (a, b) in enumerate(offsets):
        high, low = split(inv[plus(x, a), plus(y, b)])
        k.inv_parts[i * rows : (i + 1) * rows] = high
        k.inv_parts[COARSE + i * rows : COARSE + (i + 1) * rows] = low
    k.w_parts[...] = dot(k.inv_parts[...], pick).astype(bf16)

    for copy in to_two:
        copy.wait_recv()
    for c in range(4):
        cells = slice(c * BCELL, (c + 1) * BCELL)
        landed = gathered(land, halves(k.got_two[c]))
        for b in range(NB2):
            k.f_low[b, cells, :] = k.f_low[b, cells, :] + landed[b * BCELL : (b + 1) * BCELL]

    vectors = [halves(k.f_low[b]) for b in range(NB2)]
    for b in range(NB2):
        k.p_low[b] = halves(product(k.pq_low[b, 2 * UNK :], vectors[b]))

    shares = product(k.w_parts[...], k.p_low[...].reshape(NB2 * UNK, 2 * R))
    scattered = []
    for i, (a, b) in enumerate(offsets[:-1]):
        k.shares[i] = shares[i * rows : (i + 1) * rows]
        copy = to_cross(
            k.shares.at[i], k.slots.at[i], k.rs_send.at[i], k.rs_recv.at[i], plus(x, a), plus(y, b)
        )
        copy.start()
        scattered.append(copy)
    for b in range(NB2):
        y_low[b] = product(k.pq_low[b, : 2 * UNK], vectors[b])
    total = shares[COARSE - rows :]
    for i in reversed(range(n_cross - 1)):
        scattered[i].wait_recv()
        total = total + k.slots[i]
    fix[...] = total
    for copy in to_one + to_two + first + second + scattered:
        copy.wait_send()


def write(*refs):
    count = len(refs) // 2
    sems = refs[-1]
    copies = [pltpu.make_async_copy(refs[i], refs[count + i], sems.at[i]) for i in range(count)]
    for copy in copies:
        copy.start()
    for copy in copies:
        copy.wait()


def on_device(n_stream, n_cross, forcing, block_fine, couple_fine, pattern_fine, restrict_fine, landing_one,
              block_mid, couple_mid, pattern_mid, restrict_mid, landing_two, block_low, owner_cells, coarse_inverse):
    side = math.isqrt(n_cross)
    rows = COARSE // n_cross
    anywhere = pl.BlockSpec(memory_space=pl.ANY)
    hbm = pl.BlockSpec(memory_space=pltpu.HBM)
    scratch = scratch_of(side)
    shapes = (
        jax.ShapeDtypeStruct((NB0, UNK, R), f32),
        jax.ShapeDtypeStruct((NB1, UNK, R), f32),
        jax.ShapeDtypeStruct((NB2, UNK, R), f32),
        jax.ShapeDtypeStruct((rows, R), f32),
    )
    made = pl.pallas_call(
        functools.partial(kernel, n_stream, side, tuple(scratch)),
        out_shape=shapes,
        in_specs=[hbm] * 14,
        out_specs=(pl.BlockSpec(memory_space=pltpu.VMEM),) * 4,
        scratch_shapes=list(scratch.values()),
        compiler_params=pltpu.CompilerParams(
            collective_id=0, has_side_effects=True, vmem_limit_bytes=48 << 20
        ),
        name="vcycle",
    )(*(pltpu.with_memory_space_constraint(v, pltpu.HBM) for v in (
        pattern_fine[0],
        pattern_mid[0],
        restrict_fine[0],
        landing_one[0],
        restrict_mid[0],
        landing_two[0],
        owner_cells[0],
        forcing[0, 0],
        block_fine[0, 0],
        couple_fine[0, 0],
        block_mid[0, 0],
        couple_mid[0, 0],
        block_low[0, 0],
        coarse_inverse[0],
        )))
    fine, mid, low, fix = pl.pallas_call(
        write,
        out_shape=shapes,
        in_specs=[pl.BlockSpec(memory_space=pltpu.VMEM)] * 4,
        out_specs=(hbm,) * 4,
        scratch_shapes=[pltpu.SemaphoreType.DMA((4,))],
        name="write",
    )(*(pltpu.with_memory_space_constraint(v, pltpu.VMEM) for v in made))
    return fine[None, None], mid[None, None], low[None, None], fix[None]


def solution(mesh):
    tile = P("stream", "cross", None, None, None)
    table = P("stream", "cross", None)
    return jax.shard_map(
        functools.partial(on_device, mesh.shape["stream"], mesh.shape["cross"]),
        mesh=mesh,
        in_specs=(tile, tile, tile, table, table, table, tile, tile, table, table, table, tile, table, table),
        out_specs=(tile, tile, tile, table),
        check_vma=False,
    )
```

```python
import functools
import math
import types

import jax
import jax.numpy as jnp
from jax import lax
from jax.experimental import pallas as pl
from jax.experimental.pallas import tpu as pltpu
from jax.sharding import PartitionSpec as P

MESH = pl.DeviceIdType.MESH
BCELL = 32
CHEB = 6
M1 = 128
S1 = 32
M2 = 64
S2 = 16
UNK = 128
R = 128
NB0 = 8
NB1 = 4
NB2 = 2
COARSE = 512
BARRIER_AFTER = 0
LOADS = 4

centre = 1.0
spread = 0.5
coarse_weight = 0.5

f32 = jnp.float32
bf16 = jnp.bfloat16


def coefficients():
    ratio_bound = centre / spread
    momentum = 1.0 / ratio_bound
    pairs = []
    for _ in range(CHEB):
        momentum_next = 1.0 / (2.0 * ratio_bound - momentum)
        pairs.append((momentum_next * momentum, 2.0 * momentum_next / spread))
        momentum = momentum_next
    return pairs


STEPS = coefficients()


def dot(a, b):
    return jnp.dot(a, b, preferred_element_type=f32)


def split(value):
    high = value.astype(bf16)
    return high, (value - high.astype(f32)).astype(bf16)


def halves(value):
    return jnp.concatenate(split(value), axis=1)


def product(matrix, vector):
    rows = matrix.shape[0] // 2
    both = dot(matrix[:rows], vector)
    return both[:, :R] + both[:, R:] + dot(matrix[rows:], vector[:, :R])


def stack_parts(target, b, column, value):
    high, low = split(value)
    target[b, :UNK, column : column + UNK] = high
    target[b, UNK:, column : column + UNK] = low


def smoothing(blocks, pattern, source, operator, vectors, answer, residual, update, after, finish):
    for step in range(CHEB + 1):
        now, later = vectors[step % 2], vectors[(step + 1) % 2]
        for b in range(blocks):
            own = now[b]
            if pattern is not None:
                own = jnp.concatenate([own, now[pattern[b]]], axis=0)
            left = (source[b] if step == 0 else residual[b]) - product(operator[b], own)
            if step == CHEB:
                finish(b, left)
                continue
            residual[b] = left
            keep, gain = STEPS[step]
            changed = keep * (source[b] if step == 0 else update[b]) + gain * left
            if step < CHEB - 1:
                update[b] = changed
            answer[b] = (source[b] if step == 0 else answer[b]) + changed
            later[b] = halves(changed)
        after(step)


def selector(rows, targets, weight):
    wanted = lax.broadcasted_iota(jnp.int32, (rows, targets.shape[1]), 0)
    return jnp.where(wanted == targets, jnp.float32(weight), jnp.float32(0.0)).astype(bf16)


def gathered(matrix, vector):
    both = dot(matrix, vector)
    return both[:, :R] + both[:, R:]


def scratch_of(side):
    rows = COARSE // (side * side)

    def vector(blocks):
        return pltpu.VMEM((blocks, UNK, R), f32)

    def operator(blocks):
        return pltpu.VMEM((blocks, 2 * UNK, 2 * UNK), bf16)

    def parts(blocks):
        return pltpu.VMEM((blocks, UNK, 2 * R), bf16)

    def table(width):
        return pltpu.VMEM((1, width), jnp.int32)

    def dma(*shape):
        return pltpu.SemaphoreType.DMA(shape)

    return dict(
        pat_fine=pltpu.SMEM((1, NB0), jnp.int32),
        pat_mid=pltpu.SMEM((1, NB1), jnp.int32),
        map_fine=table(2 * M1),
        map_land_one=table(S1),
        map_mid=table(M1),
        map_land_two=table(S2),
        map_owner=table(M2),
        f_fine=vector(NB0),
        d_fine=vector(NB0),
        c_fine=vector(NB0),
        r_fine=vector(NB0),
        u_fine=vector(NB0),
        a_fine=operator(NB0),
        v_fine0=parts(NB0),
        v_fine1=parts(NB0),
        p_fine=parts(NB0),
        f_mid=vector(NB1),
        d_mid=vector(NB1),
        c_mid=vector(NB1),
        r_mid=vector(NB1),
        u_mid=vector(NB1),
        a_mid=operator(NB1),
        v_mid0=parts(NB1),
        v_mid1=parts(NB1),
        p_mid=parts(NB1),
        f_low=vector(NB2),
        d_low=vector(NB2),
        e_low=vector(NB2),
        x_low=vector(NB2),
        r_low=vector(NB2),
        u_low=vector(NB2),
        a_low=pltpu.VMEM((NB2, 2 * UNK, UNK), bf16),
        pq_low=pltpu.VMEM((NB2, 4 * UNK, UNK), bf16),
        v_low0=parts(NB2),
        v_low1=parts(NB2),
        p_low=parts(NB2),
        inv=pltpu.VMEM((side, side, rows, COARSE), f32),
        send_one=pltpu.VMEM((4, S1, R), f32),
        got_one=pltpu.VMEM((4, S1, R), f32),
        send_two=pltpu.VMEM((4, S2, R), f32),
        got_two=pltpu.VMEM((4, S2, R), f32),
        inv_parts=pltpu.VMEM((2 * COARSE, COARSE), bf16),
        w_parts=pltpu.VMEM((2 * COARSE, NB2 * UNK), bf16),
        shares=pltpu.VMEM((side * side, rows, R), f32),
        slots=pltpu.VMEM((side * side, rows, R), f32),
        load_small=dma(7),
        load_d=dma(LOADS),
        load_c=dma(LOADS),
        load_rest=dma(5),
        one_send=dma(4),
        one_recv=dma(4),
        two_send=dma(4),
        two_recv=dma(4),
        in_send=dma(2, 2, side),
        in_recv=dma(2, 2, side),
        on_send=dma(2, side, side),
        on_recv=dma(2, side, side),
        rs_send=dma(side * side),
        rs_recv=dma(side * side),
    )


def kernel(
    n_stream,
    side,
    names,
    pattern_fine,
    pattern_mid,
    restrict_fine,
    landing_one,
    restrict_mid,
    landing_two,
    owner_cells,
    forcing,
    block_fine,
    couple_fine,
    block_mid,
    couple_mid,
    block_low,
    inverse,
    x_fine,
    x_mid,
    y_low,
    fix,
    *scratch,
):
    k = types.SimpleNamespace(**dict(zip(names, scratch)))
    n_cross = side * side
    rows = COARSE // n_cross
    half = rows // 2
    me_s = lax.axis_index("stream")
    me_c = lax.axis_index("cross")
    x = me_c // side
    y = lax.rem(me_c, side)
    ahead = lax.rem(me_s + 1, n_stream)
    behind = lax.rem(me_s + n_stream - 1, n_stream)

    def plus(a, offset):
        return lax.rem(a + offset, side)

    def start(source, target, sem):
        copy = pltpu.make_async_copy(source, target, sem)
        copy.start()
        return copy

    def to_cross(source, target, send, recv, peer_x, peer_y):
        return pltpu.make_async_remote_copy(
            src_ref=source,
            dst_ref=target,
            send_sem=send,
            recv_sem=recv,
            device_id={"cross": peer_x * side + peer_y},
            device_id_type=MESH,
        )

    def to_next(c, source, target, send_sems, recv_sems):
        return pltpu.make_async_remote_copy(
            src_ref=source.at[c],
            dst_ref=target.at[c],
            send_sem=send_sems.at[c],
            recv_sem=recv_sems.at[c],
            device_id={"stream": ahead},
            device_id_type=MESH,
        )

    copy_f = start(forcing, k.f_fine, k.load_rest.at[4])
    copies = []
    for i in range(LOADS):
        part = pl.ds(i * NB0 // LOADS, NB0 // LOADS)
        copies.append(start(block_fine.at[part], k.d_fine.at[part], k.load_d.at[i]))
        copies.append(start(couple_fine.at[part], k.c_fine.at[part], k.load_c.at[i]))

    barrier = pltpu.get_barrier_semaphore()
    for peer in (ahead, behind):
        pl.semaphore_signal(barrier, inc=1, device_id={"stream": peer}, device_id_type=MESH)
    for o in range(1, side):
        for peer in (plus(x, o) * side + y, x * side + plus(y, o)):
            pl.semaphore_signal(barrier, inc=1, device_id={"cross": peer}, device_id_type=MESH)

    tables = (
        (pattern_fine, k.pat_fine),
        (restrict_fine, k.map_fine),
        (pattern_mid, k.pat_mid),
        (landing_one, k.map_land_one),
        (restrict_mid, k.map_mid),
        (landing_two, k.map_land_two),
        (owner_cells, k.map_owner),
    )
    small = [start(source, target, k.load_small.at[i]) for i, (source, target) in enumerate(tables)]
    inv = k.inv
    copy_inv = start(inverse, inv.at[x, y], k.load_rest.at[3])
    copy_dm = start(block_mid, k.d_mid, k.load_rest.at[0])
    copy_cm = start(couple_mid, k.c_mid, k.load_rest.at[1])
    copy_dl = start(block_low, k.d_low, k.load_rest.at[2])

    copy_f.wait()
    for b in range(NB0):
        k.v_fine0[b] = halves(k.f_fine[b])
    for i in range(LOADS):
        copies[2 * i].wait()
        copies[2 * i + 1].wait()
        for b in range(i * NB0 // LOADS, (i + 1) * NB0 // LOADS):
            stack_parts(k.a_fine, b, 0, k.d_fine[b])
            stack_parts(k.a_fine, b, UNK, k.c_fine[b])
    for copy in small:
        copy.wait()
    copy_inv.wait()

    legs = (slice(0, half), slice(half, rows))
    first, second = [], []

    def line_copies(o, kind):
        along_x = inv.at[x, y, legs[kind]]
        along_y = inv.at[x, y, legs[1 - kind]]
        return (
            to_cross(along_x, along_x, k.in_send.at[kind, 0, o], k.in_recv.at[kind, 0, o], plus(x, o), y),
            to_cross(along_y, along_y, k.in_send.at[kind, 1, o], k.in_recv.at[kind, 1, o], x, plus(y, o)),
        )

    def line_arrived(o, kind):
        along_x = inv.at[plus(x, side - o), y, legs[kind]]
        along_y = inv.at[x, plus(y, side - o), legs[1 - kind]]
        to_cross(along_x, along_x, k.in_send.at[kind, 0, o], k.in_recv.at[kind, 0, o], plus(x, o), y).wait_recv()
        to_cross(along_y, along_y, k.in_send.at[kind, 1, o], k.in_recv.at[kind, 1, o], x, plus(y, o)).wait_recv()

    def first_leg():
        for kind in range(2):
            for o in (2, 1, 3):
                first.extend(line_copies(o, kind))
        for copy in first:
            copy.start()

    def second_leg():
        for o in (1, 3, 2):
            back_x, back_y = plus(x, side - o), plus(y, side - o)
            line_arrived(o, 0)
            for p in (2, 1, 3):
                block = inv.at[back_x, y, legs[0]]
                copy = to_cross(block, block, k.on_send.at[0, o, p], k.on_recv.at[0, o, p], x, plus(y, p))
                copy.start()
                second.append(copy)
                block = inv.at[x, back_y, legs[1]]
                copy = to_cross(block, block, k.on_send.at[1, o, p], k.on_recv.at[1, o, p], plus(x, p), y)
                copy.start()
                second.append(copy)

    def second_leg_arrived():
        for o in (1, 3, 2):
            for p in (2, 1, 3):
                block = inv.at[plus(x, side - o), plus(y, side - p), legs[0]]
                to_cross(block, block, k.on_send.at[0, o, p], k.on_recv.at[0, o, p], x, plus(y, p)).wait_recv()
                block = inv.at[plus(x, side - p), plus(y, side - o), legs[1]]
                to_cross(block, block, k.on_send.at[1, o, p], k.on_recv.at[1, o, p], plus(x, p), y).wait_recv()

    def after_fine(step):
        if step == BARRIER_AFTER:
            pl.semaphore_wait(barrier, 2 * side)
            first_leg()

    def finish_fine(b, value):
        k.p_fine[b] = halves(value)

    smoothing(
        NB0, [k.pat_fine[0, b] for b in range(NB0)], k.f_fine, k.a_fine, (k.v_fine0, k.v_fine1),
        x_fine, k.r_fine, k.u_fine, after_fine, finish_fine,
    )

    def component(p, c):
        blocks = p.shape[0]
        return p[:, c * BCELL : (c + 1) * BCELL, :].reshape(blocks * BCELL, 2 * R)

    def send_straddling(p, table, owned, straddling, target, got, send_sems, recv_sems):
        pick = selector(straddling, table - owned, coarse_weight)
        for c in range(4):
            target[c] = gathered(pick, component(p, c))
        sent = [to_next(c, target, got, send_sems, recv_sems) for c in range(4)]
        for copy in sent:
            copy.start()
        return sent

    def keep_owned(p, table, owned, target):
        pick = selector(owned, table, coarse_weight)
        for c in range(4):
            sums = gathered(pick, component(p, c))
            for b in range(owned // BCELL):
                target[b, c * BCELL : (c + 1) * BCELL, :] = sums[b * BCELL : (b + 1) * BCELL]

    to_one = send_straddling(
        k.p_fine, k.map_fine[...], M1, S1, k.send_one, k.got_one, k.one_send, k.one_recv
    )
    keep_owned(k.p_fine, k.map_fine[...], M1, k.f_mid)

    copy_dm.wait()
    copy_cm.wait()
    for b in range(NB1):
        stack_parts(k.a_mid, b, 0, k.d_mid[b])
        stack_parts(k.a_mid, b, UNK, k.c_mid[b])
    second_leg()
    copy_dl.wait()
    row = lax.broadcasted_iota(jnp.int32, (UNK, UNK), 0)
    column = lax.broadcasted_iota(jnp.int32, (UNK, UNK), 1)
    for b in range(NB2):
        stack_parts(k.a_low, b, 0, k.d_low[b])
        k.e_low[b] = jnp.where(row == column, jnp.float32(1.0), jnp.float32(0.0))
        k.v_low0[b] = halves(k.e_low[b])

    def finish_low(b, value):
        high, low = split(k.x_low[b])
        k.pq_low[b, 0:UNK] = high
        k.pq_low[b, UNK : 2 * UNK] = low
        high, low = split(value)
        k.pq_low[b, 2 * UNK : 3 * UNK] = high
        k.pq_low[b, 3 * UNK :] = low

    smoothing(
        NB2, None, k.e_low, k.a_low, (k.v_low0, k.v_low1),
        k.x_low, k.r_low, k.u_low, lambda step: None, finish_low,
    )
    land = selector(M1, k.map_land_one[...], 1.0)

    for copy in to_one:
        copy.wait_recv()
    for c in range(4):
        cells = slice(c * BCELL, (c + 1) * BCELL)
        landed = gathered(land, halves(k.got_one[c]))
        for b in range(NB1):
            source = k.f_mid[b, cells, :] + landed[b * BCELL : (b + 1) * BCELL]
            k.f_mid[b, cells, :] = source
            k.v_mid0[b, cells, :] = halves(source)

    def finish_mid(b, value):
        k.p_mid[b] = halves(value)

    smoothing(
        NB1, [k.pat_mid[0, b] for b in range(NB1)], k.f_mid, k.a_mid, (k.v_mid0, k.v_mid1),
        x_mid, k.r_mid, k.u_mid, lambda step: None, finish_mid,
    )

    to_two = send_straddling(
        k.p_mid, k.map_mid[...], M2, S2, k.send_two, k.got_two, k.two_send, k.two_recv
    )
    keep_owned(k.p_mid, k.map_mid[...], M2, k.f_low)
    land = selector(M2, k.map_land_two[...], 1.0)

    owners = k.map_owner[...] * 4
    targets = jnp.concatenate(
        [owners[:, b * BCELL : (b + 1) * BCELL] + c for b in range(NB2) for c in range(4)],
        axis=1,
    )
    pick = selector(COARSE, targets, coarse_weight)
    offsets = [(a, b) for a in range(side) for b in range(side)]
    offsets.sort(key=lambda o: (o[0] * o[1] == 0, -min(o[0], side - o[0]) - min(o[1], side - o[1])))
    far = (side - 1) * (side - 1)

    def fold(begin, end):
        count = (end - begin) * rows
        for i in range(begin, end):
            high, low = split(inv[plus(x, offsets[i][0]), plus(y, offsets[i][1])])
            at = (i - begin) * rows
            k.inv_parts[at : at + rows] = high
            k.inv_parts[count + at : count + at + rows] = low
        both = dot(k.inv_parts[: 2 * count], pick).astype(bf16)
        k.w_parts[2 * begin * rows : 2 * end * rows] = both

    for o in (1, 3, 2):
        line_arrived(o, 1)
    fold(far, n_cross)
    second_leg_arrived()
    fold(0, far)

    for copy in to_two:
        copy.wait_recv()
    for c in range(4):
        cells = slice(c * BCELL, (c + 1) * BCELL)
        landed = gathered(land, halves(k.got_two[c]))
        for b in range(NB2):
            k.f_low[b, cells, :] = k.f_low[b, cells, :] + landed[b * BCELL : (b + 1) * BCELL]

    vectors = [halves(k.f_low[b]) for b in range(NB2)]
    for b in range(NB2):
        k.p_low[b] = halves(product(k.pq_low[b, 2 * UNK :], vectors[b]))

    vector = k.p_low[...].reshape(NB2 * UNK, 2 * R)
    scattered = []
    for begin, end in ((0, far), (far, n_cross)):
        shares = product(k.w_parts[2 * begin * rows : 2 * end * rows], vector)
        for i in range(begin, min(end, n_cross - 1)):
            k.shares[i] = shares[(i - begin) * rows : (i - begin + 1) * rows]
            copy = to_cross(
                k.shares.at[i],
                k.slots.at[i],
                k.rs_send.at[i],
                k.rs_recv.at[i],
                plus(x, offsets[i][0]),
                plus(y, offsets[i][1]),
            )
            copy.start()
            scattered.append(copy)
    total = shares[(n_cross - 1 - far) * rows :]
    for b in range(NB2):
        y_low[b] = product(k.pq_low[b, : 2 * UNK], vectors[b])
    for i in reversed(range(n_cross - 1)):
        scattered[i].wait_recv()
        total = total + k.slots[i]
    fix[...] = total
    for copy in to_one + to_two + first + second + scattered:
        copy.wait_send()


def write(*refs):
    count = len(refs) // 2
    sems = refs[-1]
    copies = [pltpu.make_async_copy(refs[i], refs[count + i], sems.at[i]) for i in range(count)]
    for copy in copies:
        copy.start()
    for copy in copies:
        copy.wait()


def on_device(n_stream, n_cross, forcing, block_fine, couple_fine, pattern_fine, restrict_fine, landing_one,
              block_mid, couple_mid, pattern_mid, restrict_mid, landing_two, block_low, owner_cells, coarse_inverse):
    side = math.isqrt(n_cross)
    rows = COARSE // n_cross
    anywhere = pl.BlockSpec(memory_space=pl.ANY)
    hbm = pl.BlockSpec(memory_space=pltpu.HBM)
    scratch = scratch_of(side)
    shapes = (
        jax.ShapeDtypeStruct((NB0, UNK, R), f32),
        jax.ShapeDtypeStruct((NB1, UNK, R), f32),
        jax.ShapeDtypeStruct((NB2, UNK, R), f32),
        jax.ShapeDtypeStruct((rows, R), f32),
    )
    made = pl.pallas_call(
        functools.partial(kernel, n_stream, side, tuple(scratch)),
        out_shape=shapes,
        in_specs=[hbm] * 14,
        out_specs=(pl.BlockSpec(memory_space=pltpu.VMEM),) * 4,
        scratch_shapes=list(scratch.values()),
        compiler_params=pltpu.CompilerParams(
            collective_id=0, has_side_effects=True, vmem_limit_bytes=48 << 20
        ),
        name="vcycle",
    )(*(pltpu.with_memory_space_constraint(v, pltpu.HBM) for v in (
        pattern_fine[0],
        pattern_mid[0],
        restrict_fine[0],
        landing_one[0],
        restrict_mid[0],
        landing_two[0],
        owner_cells[0],
        forcing[0, 0],
        block_fine[0, 0],
        couple_fine[0, 0],
        block_mid[0, 0],
        couple_mid[0, 0],
        block_low[0, 0],
        coarse_inverse[0],
        )))
    fine, mid, low, fix = pl.pallas_call(
        write,
        out_shape=shapes,
        in_specs=[pl.BlockSpec(memory_space=pltpu.VMEM)] * 4,
        out_specs=(hbm,) * 4,
        scratch_shapes=[pltpu.SemaphoreType.DMA((4,))],
        name="write",
    )(*(pltpu.with_memory_space_constraint(v, pltpu.VMEM) for v in made))
    return fine[None, None], mid[None, None], low[None, None], fix[None]


def solution(mesh):
    tile = P("stream", "cross", None, None, None)
    table = P("stream", "cross", None)
    return jax.shard_map(
        functools.partial(on_device, mesh.shape["stream"], mesh.shape["cross"]),
        mesh=mesh,
        in_specs=(tile, tile, tile, table, table, table, tile, tile, table, table, table, tile, table, table),
        out_specs=(tile, tile, tile, table),
        check_vma=False,
    )
```

```python
import functools
import math
import types

import jax
import jax.numpy as jnp
from jax import lax
from jax.experimental import pallas as pl
from jax.experimental.pallas import tpu as pltpu
from jax.sharding import PartitionSpec as P

MESH = pl.DeviceIdType.MESH
BCELL = 32
CHEB = 6
M1 = 128
S1 = 32
M2 = 64
S2 = 16
UNK = 128
R = 128
NB0 = 8
NB1 = 4
NB2 = 2
COARSE = 512
BARRIER_AFTER = 0
LOADS = 1

centre = 1.0
spread = 0.5
coarse_weight = 0.5

f32 = jnp.float32
bf16 = jnp.bfloat16


def coefficients():
    ratio_bound = centre / spread
    momentum = 1.0 / ratio_bound
    pairs = []
    for _ in range(CHEB):
        momentum_next = 1.0 / (2.0 * ratio_bound - momentum)
        pairs.append((momentum_next * momentum, 2.0 * momentum_next / spread))
        momentum = momentum_next
    return pairs


STEPS = coefficients()


def dot(a, b):
    return jnp.dot(a, b, preferred_element_type=f32)


def split(value):
    high = value.astype(bf16)
    return high, (value - high.astype(f32)).astype(bf16)


def halves(value):
    return jnp.concatenate(split(value), axis=1)


def product(matrix, vector):
    rows = matrix.shape[0] // 2
    both = dot(matrix[:rows], vector)
    return both[:, :R] + both[:, R:] + dot(matrix[rows:], vector[:, :R])


def stack_parts(target, b, column, value):
    high, low = split(value)
    target[b, :UNK, column : column + UNK] = high
    target[b, UNK:, column : column + UNK] = low


def smoothing(blocks, pattern, source, operator, vectors, answer, residual, update, after, finish):
    for step in range(CHEB + 1):
        now, later = vectors[step % 2], vectors[(step + 1) % 2]
        for b in range(blocks):
            own = now[b]
            if pattern is not None:
                own = jnp.concatenate([own, now[pattern[b]]], axis=0)
            left = (source[b] if step == 0 else residual[b]) - product(operator[b], own)
            if step == CHEB:
                finish(b, left)
                continue
            residual[b] = left
            keep, gain = STEPS[step]
            last = source[b] if step == 0 else update[b]
            changed = keep * last + gain * left
            later[b] = halves(changed)
            if step < CHEB - 1:
                update[b] = changed
            if step % 2 == 1:
                answer[b] = (source[b] if step == 1 else answer[b]) + (last + changed)
        after(step)


def selector(rows, targets, weight):
    wanted = lax.broadcasted_iota(jnp.int32, (rows, targets.shape[1]), 0)
    return jnp.where(wanted == targets, jnp.float32(weight), jnp.float32(0.0)).astype(bf16)


def gathered(matrix, vector):
    both = dot(matrix, vector)
    return both[:, :R] + both[:, R:]


def scratch_of(side):
    rows = COARSE // (side * side)

    def vector(blocks):
        return pltpu.VMEM((blocks, UNK, R), f32)

    def operator(blocks):
        return pltpu.VMEM((blocks, 2 * UNK, 2 * UNK), bf16)

    def parts(blocks):
        return pltpu.VMEM((blocks, UNK, 2 * R), bf16)

    def table(width):
        return pltpu.VMEM((1, width), jnp.int32)

    def dma(*shape):
        return pltpu.SemaphoreType.DMA(shape)

    return dict(
        pat_fine=pltpu.SMEM((1, NB0), jnp.int32),
        pat_mid=pltpu.SMEM((1, NB1), jnp.int32),
        map_fine=table(2 * M1),
        map_land_one=table(S1),
        map_mid=table(M1),
        map_land_two=table(S2),
        map_owner=table(M2),
        f_fine=vector(NB0),
        d_fine=vector(NB0),
        c_fine=vector(NB0),
        r_fine=vector(NB0),
        u_fine=vector(NB0),
        a_fine=operator(NB0),
        v_fine0=parts(NB0),
        v_fine1=parts(NB0),
        p_fine=parts(NB0),
        f_mid=vector(NB1),
        d_mid=vector(NB1),
        c_mid=vector(NB1),
        r_mid=vector(NB1),
        u_mid=vector(NB1),
        a_mid=operator(NB1),
        v_mid0=parts(NB1),
        v_mid1=parts(NB1),
        p_mid=parts(NB1),
        f_low=vector(NB2),
        d_low=vector(NB2),
        e_low=vector(NB2),
        x_low=vector(NB2),
        r_low=vector(NB2),
        u_low=vector(NB2),
        a_low=pltpu.VMEM((NB2, 2 * UNK, UNK), bf16),
        pq_low=pltpu.VMEM((NB2, 4 * UNK, UNK), bf16),
        v_low0=parts(NB2),
        v_low1=parts(NB2),
        p_low=parts(NB2),
        inv=pltpu.VMEM((side, side, rows, COARSE), f32),
        send_one=pltpu.VMEM((4, S1, R), f32),
        got_one=pltpu.VMEM((4, S1, R), f32),
        send_two=pltpu.VMEM((4, S2, R), f32),
        got_two=pltpu.VMEM((4, S2, R), f32),
        inv_parts=pltpu.VMEM((2 * COARSE, COARSE), bf16),
        w_parts=pltpu.VMEM((2 * COARSE, NB2 * UNK), bf16),
        shares=pltpu.VMEM((side * side, rows, R), f32),
        slots=pltpu.VMEM((side * side, rows, R), f32),
        load_small=dma(7),
        load_d=dma(LOADS),
        load_c=dma(LOADS),
        load_rest=dma(5),
        one_send=dma(4),
        one_recv=dma(4),
        two_send=dma(4),
        two_recv=dma(4),
        in_send=dma(2, 2, side),
        in_recv=dma(2, 2, side),
        on_send=dma(2, side, side),
        on_recv=dma(2, side, side),
        rs_send=dma(side * side),
        rs_recv=dma(side * side),
    )


def kernel(
    n_stream,
    side,
    names,
    pattern_fine,
    pattern_mid,
    restrict_fine,
    landing_one,
    restrict_mid,
    landing_two,
    owner_cells,
    forcing,
    block_fine,
    couple_fine,
    block_mid,
    couple_mid,
    block_low,
    inverse,
    x_fine,
    x_mid,
    y_low,
    fix,
    *scratch,
):
    k = types.SimpleNamespace(**dict(zip(names, scratch)))
    n_cross = side * side
    rows = COARSE // n_cross
    half = rows // 2
    me_s = lax.axis_index("stream")
    me_c = lax.axis_index("cross")
    x = me_c // side
    y = lax.rem(me_c, side)
    ahead = lax.rem(me_s + 1, n_stream)
    behind = lax.rem(me_s + n_stream - 1, n_stream)

    def plus(a, offset):
        return lax.rem(a + offset, side)

    def start(source, target, sem):
        copy = pltpu.make_async_copy(source, target, sem)
        copy.start()
        return copy

    def to_cross(source, target, send, recv, peer_x, peer_y):
        return pltpu.make_async_remote_copy(
            src_ref=source,
            dst_ref=target,
            send_sem=send,
            recv_sem=recv,
            device_id={"cross": peer_x * side + peer_y},
            device_id_type=MESH,
        )

    def to_next(c, source, target, send_sems, recv_sems):
        return pltpu.make_async_remote_copy(
            src_ref=source.at[c],
            dst_ref=target.at[c],
            send_sem=send_sems.at[c],
            recv_sem=recv_sems.at[c],
            device_id={"stream": ahead},
            device_id_type=MESH,
        )

    copy_f = start(forcing, k.f_fine, k.load_rest.at[4])
    copies = []
    for i in range(LOADS):
        part = pl.ds(i * NB0 // LOADS, NB0 // LOADS)
        copies.append(start(block_fine.at[part], k.d_fine.at[part], k.load_d.at[i]))
        copies.append(start(couple_fine.at[part], k.c_fine.at[part], k.load_c.at[i]))

    barrier = pltpu.get_barrier_semaphore()
    pl.semaphore_signal(barrier, inc=1, device_id={"stream": behind}, device_id_type=MESH)
    for o in range(1, side):
        for peer in (plus(x, o) * side + y, x * side + plus(y, o)):
            pl.semaphore_signal(barrier, inc=1, device_id={"cross": peer}, device_id_type=MESH)

    tables = (
        (pattern_fine, k.pat_fine),
        (restrict_fine, k.map_fine),
        (pattern_mid, k.pat_mid),
        (landing_one, k.map_land_one),
        (restrict_mid, k.map_mid),
        (landing_two, k.map_land_two),
        (owner_cells, k.map_owner),
    )
    small = [start(source, target, k.load_small.at[i]) for i, (source, target) in enumerate(tables)]
    inv = k.inv
    copy_inv = start(inverse, inv.at[x, y], k.load_rest.at[3])
    copy_dm = start(block_mid, k.d_mid, k.load_rest.at[0])
    copy_cm = start(couple_mid, k.c_mid, k.load_rest.at[1])
    copy_dl = start(block_low, k.d_low, k.load_rest.at[2])

    copy_f.wait()
    for b in range(NB0):
        k.v_fine0[b] = halves(k.f_fine[b])
    for i in range(LOADS):
        copies[2 * i].wait()
        copies[2 * i + 1].wait()
        for b in range(i * NB0 // LOADS, (i + 1) * NB0 // LOADS):
            stack_parts(k.a_fine, b, 0, k.d_fine[b])
            stack_parts(k.a_fine, b, UNK, k.c_fine[b])
    for copy in small:
        copy.wait()
    copy_inv.wait()

    legs = (slice(0, half), slice(half, rows))
    first, second = [], []

    def line_copies(o, kind):
        along_x = inv.at[x, y, legs[kind]]
        along_y = inv.at[x, y, legs[1 - kind]]
        return (
            to_cross(along_x, along_x, k.in_send.at[kind, 0, o], k.in_recv.at[kind, 0, o], plus(x, o), y),
            to_cross(along_y, along_y, k.in_send.at[kind, 1, o], k.in_recv.at[kind, 1, o], x, plus(y, o)),
        )

    def line_arrived(o, kind):
        along_x = inv.at[plus(x, side - o), y, legs[kind]]
        along_y = inv.at[x, plus(y, side - o), legs[1 - kind]]
        to_cross(along_x, along_x, k.in_send.at[kind, 0, o], k.in_recv.at[kind, 0, o], plus(x, o), y).wait_recv()
        to_cross(along_y, along_y, k.in_send.at[kind, 1, o], k.in_recv.at[kind, 1, o], x, plus(y, o)).wait_recv()

    def first_leg():
        for kind in range(2):
            for o in (2, 1, 3):
                first.extend(line_copies(o, kind))
        for copy in first:
            copy.start()

    def second_leg():
        for o in (1, 3, 2):
            back_x, back_y = plus(x, side - o), plus(y, side - o)
            line_arrived(o, 0)
            for p in (2, 1, 3):
                block = inv.at[back_x, y, legs[0]]
                copy = to_cross(block, block, k.on_send.at[0, o, p], k.on_recv.at[0, o, p], x, plus(y, p))
                copy.start()
                second.append(copy)
                block = inv.at[x, back_y, legs[1]]
                copy = to_cross(block, block, k.on_send.at[1, o, p], k.on_recv.at[1, o, p], plus(x, p), y)
                copy.start()
                second.append(copy)

    def second_leg_arrived():
        for o in (1, 3, 2):
            for p in (2, 1, 3):
                block = inv.at[plus(x, side - o), plus(y, side - p), legs[0]]
                to_cross(block, block, k.on_send.at[0, o, p], k.on_recv.at[0, o, p], x, plus(y, p)).wait_recv()
                block = inv.at[plus(x, side - p), plus(y, side - o), legs[1]]
                to_cross(block, block, k.on_send.at[1, o, p], k.on_recv.at[1, o, p], plus(x, p), y).wait_recv()

    def after_fine(step):
        if step == BARRIER_AFTER:
            pl.semaphore_wait(barrier, 2 * side - 1)
            first_leg()

    def finish_fine(b, value):
        k.p_fine[b] = halves(value)

    smoothing(
        NB0, [k.pat_fine[0, b] for b in range(NB0)], k.f_fine, k.a_fine, (k.v_fine0, k.v_fine1),
        x_fine, k.r_fine, k.u_fine, after_fine, finish_fine,
    )

    def component(p, c):
        blocks = p.shape[0]
        return p[:, c * BCELL : (c + 1) * BCELL, :].reshape(blocks * BCELL, 2 * R)

    def send_straddling(p, table, owned, straddling, target, got, send_sems, recv_sems):
        pick = selector(straddling, table - owned, coarse_weight)
        for c in range(4):
            target[c] = gathered(pick, component(p, c))
        sent = [to_next(c, target, got, send_sems, recv_sems) for c in range(4)]
        for copy in sent:
            copy.start()
        return sent

    def keep_owned(p, table, owned, target):
        pick = selector(owned, table, coarse_weight)
        for c in range(4):
            sums = gathered(pick, component(p, c))
            for b in range(owned // BCELL):
                target[b, c * BCELL : (c + 1) * BCELL, :] = sums[b * BCELL : (b + 1) * BCELL]

    to_one = send_straddling(
        k.p_fine, k.map_fine[...], M1, S1, k.send_one, k.got_one, k.one_send, k.one_recv
    )
    keep_owned(k.p_fine, k.map_fine[...], M1, k.f_mid)

    copy_dm.wait()
    copy_cm.wait()
    for b in range(NB1):
        stack_parts(k.a_mid, b, 0, k.d_mid[b])
        stack_parts(k.a_mid, b, UNK, k.c_mid[b])
    second_leg()
    copy_dl.wait()
    row = lax.broadcasted_iota(jnp.int32, (UNK, UNK), 0)
    column = lax.broadcasted_iota(jnp.int32, (UNK, UNK), 1)
    for b in range(NB2):
        stack_parts(k.a_low, b, 0, k.d_low[b])
        k.e_low[b] = jnp.where(row == column, jnp.float32(1.0), jnp.float32(0.0))
        k.v_low0[b] = halves(k.e_low[b])

    def finish_low(b, value):
        high, low = split(k.x_low[b])
        k.pq_low[b, 0:UNK] = high
        k.pq_low[b, UNK : 2 * UNK] = low
        high, low = split(value)
        k.pq_low[b, 2 * UNK : 3 * UNK] = high
        k.pq_low[b, 3 * UNK :] = low

    smoothing(
        NB2, None, k.e_low, k.a_low, (k.v_low0, k.v_low1),
        k.x_low, k.r_low, k.u_low, lambda step: None, finish_low,
    )
    land = selector(M1, k.map_land_one[...], 1.0)

    for copy in to_one:
        copy.wait_recv()
    for c in range(4):
        cells = slice(c * BCELL, (c + 1) * BCELL)
        landed = gathered(land, halves(k.got_one[c]))
        for b in range(NB1):
            source = k.f_mid[b, cells, :] + landed[b * BCELL : (b + 1) * BCELL]
            k.f_mid[b, cells, :] = source
            k.v_mid0[b, cells, :] = halves(source)

    def finish_mid(b, value):
        k.p_mid[b] = halves(value)

    smoothing(
        NB1, [k.pat_mid[0, b] for b in range(NB1)], k.f_mid, k.a_mid, (k.v_mid0, k.v_mid1),
        x_mid, k.r_mid, k.u_mid, lambda step: None, finish_mid,
    )

    to_two = send_straddling(
        k.p_mid, k.map_mid[...], M2, S2, k.send_two, k.got_two, k.two_send, k.two_recv
    )
    keep_owned(k.p_mid, k.map_mid[...], M2, k.f_low)
    land = selector(M2, k.map_land_two[...], 1.0)

    owners = k.map_owner[...] * 4
    targets = jnp.concatenate(
        [owners[:, b * BCELL : (b + 1) * BCELL] + c for b in range(NB2) for c in range(4)],
        axis=1,
    )
    pick = selector(COARSE, targets, coarse_weight)
    offsets = [(a, b) for a in range(side) for b in range(side)]
    offsets.sort(key=lambda o: (o[0] * o[1] == 0, -min(o[0], side - o[0]) - min(o[1], side - o[1])))
    far = (side - 1) * (side - 1)

    def fold(begin, end):
        count = (end - begin) * rows
        for i in range(begin, end):
            high, low = split(inv[plus(x, offsets[i][0]), plus(y, offsets[i][1])])
            at = (i - begin) * rows
            k.inv_parts[at : at + rows] = high
            k.inv_parts[count + at : count + at + rows] = low
        both = dot(k.inv_parts[: 2 * count], pick).astype(bf16)
        k.w_parts[2 * begin * rows : 2 * end * rows] = both

    for o in (1, 3, 2):
        line_arrived(o, 1)
    fold(far, n_cross)
    second_leg_arrived()
    fold(0, far)

    for copy in to_two:
        copy.wait_recv()
    for c in range(4):
        cells = slice(c * BCELL, (c + 1) * BCELL)
        landed = gathered(land, halves(k.got_two[c]))
        for b in range(NB2):
            k.f_low[b, cells, :] = k.f_low[b, cells, :] + landed[b * BCELL : (b + 1) * BCELL]

    vectors = [halves(k.f_low[b]) for b in range(NB2)]
    for b in range(NB2):
        k.p_low[b] = halves(product(k.pq_low[b, 2 * UNK :], vectors[b]))

    vector = k.p_low[...].reshape(NB2 * UNK, 2 * R)
    scattered = []
    for begin, end in ((0, far), (far, n_cross)):
        shares = product(k.w_parts[2 * begin * rows : 2 * end * rows], vector)
        for i in range(begin, min(end, n_cross - 1)):
            k.shares[i] = shares[(i - begin) * rows : (i - begin + 1) * rows]
            copy = to_cross(
                k.shares.at[i],
                k.slots.at[i],
                k.rs_send.at[i],
                k.rs_recv.at[i],
                plus(x, offsets[i][0]),
                plus(y, offsets[i][1]),
            )
            copy.start()
            scattered.append(copy)
    total = shares[(n_cross - 1 - far) * rows :]
    for b in range(NB2):
        y_low[b] = product(k.pq_low[b, : 2 * UNK], vectors[b])
    for i in reversed(range(n_cross - 1)):
        scattered[i].wait_recv()
        total = total + k.slots[i]
    fix[...] = total
    for copy in to_one + to_two + first + second + scattered:
        copy.wait_send()


def write(*refs):
    count = len(refs) // 2
    sems = refs[-1]
    copies = [pltpu.make_async_copy(refs[i], refs[count + i], sems.at[i]) for i in range(count)]
    for copy in copies:
        copy.start()
    for copy in copies:
        copy.wait()


def on_device(n_stream, n_cross, forcing, block_fine, couple_fine, pattern_fine, restrict_fine, landing_one,
              block_mid, couple_mid, pattern_mid, restrict_mid, landing_two, block_low, owner_cells, coarse_inverse):
    side = math.isqrt(n_cross)
    rows = COARSE // n_cross
    anywhere = pl.BlockSpec(memory_space=pl.ANY)
    hbm = pl.BlockSpec(memory_space=pltpu.HBM)
    scratch = scratch_of(side)
    shapes = (
        jax.ShapeDtypeStruct((NB0, UNK, R), f32),
        jax.ShapeDtypeStruct((NB1, UNK, R), f32),
        jax.ShapeDtypeStruct((NB2, UNK, R), f32),
        jax.ShapeDtypeStruct((rows, R), f32),
    )
    made = pl.pallas_call(
        functools.partial(kernel, n_stream, side, tuple(scratch)),
        out_shape=shapes,
        in_specs=[hbm] * 14,
        out_specs=(pl.BlockSpec(memory_space=pltpu.VMEM),) * 4,
        scratch_shapes=list(scratch.values()),
        compiler_params=pltpu.CompilerParams(
            collective_id=0, has_side_effects=True, vmem_limit_bytes=48 << 20
        ),
        name="vcycle",
    )(*(pltpu.with_memory_space_constraint(v, pltpu.HBM) for v in (
        pattern_fine[0],
        pattern_mid[0],
        restrict_fine[0],
        landing_one[0],
        restrict_mid[0],
        landing_two[0],
        owner_cells[0],
        forcing[0, 0],
        block_fine[0, 0],
        couple_fine[0, 0],
        block_mid[0, 0],
        couple_mid[0, 0],
        block_low[0, 0],
        coarse_inverse[0],
        )))
    fine, mid, low, fix = pl.pallas_call(
        write,
        out_shape=shapes,
        in_specs=[pl.BlockSpec(memory_space=pltpu.VMEM)] * 4,
        out_specs=(hbm,) * 4,
        scratch_shapes=[pltpu.SemaphoreType.DMA((4,))],
        name="write",
    )(*(pltpu.with_memory_space_constraint(v, pltpu.VMEM) for v in made))
    return fine[None, None], mid[None, None], low[None, None], fix[None]


def solution(mesh):
    tile = P("stream", "cross", None, None, None)
    table = P("stream", "cross", None)
    return jax.shard_map(
        functools.partial(on_device, mesh.shape["stream"], mesh.shape["cross"]),
        mesh=mesh,
        in_specs=(tile, tile, tile, table, table, table, tile, tile, table, table, table, tile, table, table),
        out_specs=(tile, tile, tile, table),
        check_vma=False,
    )
```
